128 devices in a mesh: loop: 16 (over y_lo, z, core), red: 8 (over y_hi, x).
Axes of the slice: x: 4, y: 4 (y_hi: 2, y_lo: 2; y = y_hi * 2 + y_lo), z: 4, core: 2. Of those that a mesh axis runs over, the one named last changes fastest.
Arguments:
- query_ids: int32 [512], replicated, may hold values from 0 to 8191
- layer_index: int32 [1], replicated, may hold values from 0 to 3
- gradient: bfloat16 [8192, 28672], P('loop', 'red'), may hold values from -6 to 6
- out_basis: bfloat16 [8192, 8192], P('loop'), may hold values from -0.0625 to 0.0625
- in_basis: bfloat16 [28672, 28672], P('red', 'loop'), may hold values from -0.03125 to 0.03125
- out_eigen: float32 [4, 8192], replicated, may hold values from 0.2 to 2
- in_eigen: float32 [4, 28672], P(None, 'loop'), may hold values from 0.2 to 2
Outputs:
- preconditioned: bfloat16 [512, 28672], P('loop', 'red')
The draws below stay inside these ranges and needn't reach their ends.
All inputs are finite; a program needn't handle non-finite values.
Results may differ from the reference program's by a relative error of at most 0.0055.
Values may be sent and summed in bfloat16 or wider, within the bound.
No kernel may reach another device: no remote copies, remote signals or barrier semaphores. Data moves between devices by JAX's collectives and lax.ppermute only.
A program may use at most 128 MiB of HBM per device.

```python
import math
import jax
import jax.numpy as jnp
from jax import lax

D = 8192
FF = 28672
QUERIES = 512
LAYERS = 4


def place_ends(values, rng, low, largest):
    dims = values.shape
    index_at = [jax.random.randint(jax.random.fold_in(rng, axis), (), 0, dims[axis]) for axis in range(len(dims))]
    values = values.at[tuple(index_at)].set(low)
    longest = dims.index(max(dims))
    index_at[longest] = (index_at[longest] + 1) % dims[longest]
    return values.at[tuple(index_at)].set(largest)


def steps_of(key, dims, split, low, largest):
    level, own = 1.0, jax.random.fold_in(key, 6)
    for position, shards_of in split:
        heights = jnp.exp(jax.random.uniform(jax.random.fold_in(own, position), (shards_of,), jnp.float32, low / len(split), largest / len(split)))
        level = level * jnp.repeat(heights, dims[position] // shards_of).reshape([-1 if axis == position else 1 for axis in range(len(dims))])
    return level


def centred(key, shape, spread, most, cuts=(), dtype=jnp.bfloat16):
    values = jax.random.normal(key, shape, jnp.float32) * spread
    if len(cuts) > 0:
        values = steps_of(key, shape, cuts, -0.22, 0.18) * values
    return jnp.clip(values, min=-most, max=most).astype(dtype)


def setup_inputs(seed: int = 0) -> dict:
    splits = jax.random.split(jax.random.key(seed), 8)
    return {
        "query_ids": place_ends(jax.random.randint(splits[0], (QUERIES,), 0, D), jax.random.fold_in(splits[0], 1), 0, D - 1).astype(jnp.int32),
        "layer_index": jax.random.randint(splits[1], (1,), 0, LAYERS).astype(jnp.int32),
        "gradient": centred(splits[2], (D, FF), 1.0, 6.0, ((0, 16), (1, 8))),
        "out_basis": centred(splits[3], (D, D), D ** -0.5, 0.0625, ((0, 16),)),
        "in_basis": centred(splits[4], (FF, FF), FF ** -0.5, 0.03125, ((0, 8), (1, 16))),
        "out_eigen": jnp.clip(jnp.exp(jax.random.uniform(splits[5], (LAYERS, D), jnp.float32, math.log(0.2), math.log(2.0))), 0.2, 2.0),
        "in_eigen": jnp.clip(jnp.exp(math.log(2.0) - 2.3025851 * jax.random.uniform(splits[6], (LAYERS, FF), jnp.float32) ** steps_of(splits[6], (LAYERS, FF), ((1, 16),), -0.2, 0.2)), 0.2, 2.0),
    }


damping = 0.05


def reference(query_ids, layer_index, gradient, out_basis, in_basis, out_eigen, in_eigen):
    selected = jnp.take(out_basis, query_ids, axis=1)
    rows_w = lax.dot_general(selected, gradient, (((0,), (0,)), ((), ())), preferred_element_type=jnp.float32).astype(jnp.bfloat16)
    rotated = jnp.dot(rows_w, in_basis, preferred_element_type=jnp.float32)
    eigen_rows = jnp.take(jnp.take(out_eigen, layer_index, axis=0)[0], query_ids)
    eigen_cols = jnp.take(in_eigen, layer_index, axis=0)[0]
    scaled = (rotated / (eigen_rows[:, None] * eigen_cols[None, :] + damping)).astype(jnp.bfloat16)
    result = lax.dot_general(scaled, in_basis, (((1,), (1,)), ((), ())), preferred_element_type=jnp.float32)
    return result.astype(jnp.bfloat16)
```

```python
import functools

import jax
import jax.numpy as jnp
from jax import lax
from jax.experimental import pallas as pl
from jax.experimental.pallas import tpu as pltpu
from jax.sharding import PartitionSpec as P

damping = 0.05
CHUNKS = 2
F32, BF16 = jnp.float32, jnp.bfloat16
VMEM = pl.BlockSpec(memory_space=pltpu.VMEM)
SMEM = pl.BlockSpec(memory_space=pltpu.SMEM)
NN = (((1,), (0,)), ((), ()))
NT = (((1,), (1,)), ((), ()))


def cost(flops, nbytes):
    return pl.CostEstimate(flops=flops, bytes_accessed=nbytes, transcendentals=0)


def dot(a, b, dims=NN):
    return lax.dot_general(a, b, dims, preferred_element_type=F32)


def select_kernel(ids_ref, basis_ref, out_ref, acc_ref):
    step = pl.program_id(0)
    width = basis_ref.shape[1]
    lanes = lax.broadcasted_iota(jnp.int32, (ids_ref.shape[0], width), 1)
    hot = jnp.where(lanes + step * width == ids_ref[...], 1.0, 0.0).astype(BF16)
    part = dot(hot, basis_ref[...], NT)

    @pl.when(step == 0)
    def _():
        acc_ref[...] = part

    @pl.when(step > 0)
    def _():
        acc_ref[...] += part

    @pl.when(step == pl.num_programs(0) - 1)
    def _():
        out_ref[...] = acc_ref[...].astype(BF16)


def select(ids, basis):
    rows, width = basis.shape
    queries, block = ids.shape[0], 1024
    return pl.pallas_call(
        select_kernel,
        grid=(width // block,),
        in_specs=[
            pl.BlockSpec((queries, 1), lambda i: (0, 0)),
            pl.BlockSpec((rows, block), lambda i: (0, i)),
        ],
        out_specs=pl.BlockSpec((queries, rows), lambda i: (0, 0)),
        out_shape=jax.ShapeDtypeStruct((queries, rows), BF16),
        scratch_shapes=[pltpu.VMEM((queries, rows), F32)],
        cost_estimate=cost(2 * queries * rows * width, rows * width * 2),
        compiler_params=pltpu.CompilerParams(vmem_limit_bytes=16 << 20),
    )(ids[:, None], basis)


def pair_kernel(a1, b1, a2, b2, out, *, tile):
    for j in range(out.shape[1] // tile):
        at = pl.ds(j * tile, tile)
        out[:, at] = (dot(a1[...], b1[:, at]) + dot(a2[...], b2[:, at])).astype(out.dtype)


def pair_matmul(a1, b1, a2, b2):
    m, k = a1.shape
    n = b1.shape[1]
    return pl.pallas_call(
        functools.partial(pair_kernel, tile=256),
        in_specs=[VMEM] * 4,
        out_specs=VMEM,
        out_shape=jax.ShapeDtypeStruct((m, n), BF16),
        cost_estimate=cost(4 * m * k * n, 2 * (2 * m * k + 2 * k * n + m * n)),
        compiler_params=pltpu.CompilerParams(vmem_limit_bytes=16 << 20),
    )(a1, b1, a2, b2)


def rotate_kernel(core, own, other, basis, out, *, tile):
    half = own.shape[1]
    mine = pl.multiple_of(core[0] * half, half)
    theirs = pl.multiple_of((1 - core[0]) * half, half)
    for j in range(out.shape[1] // tile):
        at = pl.ds(j * tile, tile)
        total = dot(own[...], basis[pl.ds(mine, half), at])
        total += dot(other[...], basis[pl.ds(theirs, half), at])
        out[:, at] = total.astype(out.dtype)


def rotate(core, own, other, basis):
    m, half = own.shape
    n = basis.shape[1]
    return pl.pallas_call(
        functools.partial(rotate_kernel, tile=256),
        in_specs=[SMEM, VMEM, VMEM, VMEM],
        out_specs=VMEM,
        out_shape=jax.ShapeDtypeStruct((m, n), BF16),
        cost_estimate=cost(4 * m * half * n, 2 * (2 * m * half + 2 * half * n + m * n)),
        compiler_params=pltpu.CompilerParams(vmem_limit_bytes=32 << 20),
    )(core, own, other, basis)


def back_kernel(core, scaled, basis, other, own, *, tile):
    half = scaled.shape[0] // 2
    mine = pl.multiple_of(core[0] * half, half)
    theirs = pl.multiple_of((1 - core[0]) * half, half)
    for j in range(basis.shape[0] // tile):
        at = pl.ds(j * tile, tile)
        block = basis[at, :]
        other[:, at] = dot(scaled[pl.ds(theirs, half), :], block, NT).astype(BF16)
        own[:, at] = dot(scaled[pl.ds(mine, half), :], block, NT)


def back(core, scaled, basis):
    m, k = scaled.shape
    n = basis.shape[0]
    return pl.pallas_call(
        functools.partial(back_kernel, tile=256),
        in_specs=[SMEM, VMEM, VMEM],
        out_specs=[VMEM, VMEM],
        out_shape=[
            jax.ShapeDtypeStruct((m // 2, n), BF16),
            jax.ShapeDtypeStruct((m // 2, n), F32),
        ],
        cost_estimate=cost(2 * m * k * n, 2 * (m * k + k * n + m * n)),
        compiler_params=pltpu.CompilerParams(vmem_limit_bytes=32 << 20),
    )(core, scaled, basis)


def per_device(query_ids, layer_index, gradient, out_basis, in_basis, out_eigen, in_eigen):
    loops, reds = lax.axis_size("loop"), lax.axis_size("red")
    chips = loops // 2
    queries = query_ids.shape[0]
    chunk = queries // CHUNKS
    core = lax.axis_index("loop") % 2
    core1 = core[None].astype(jnp.int32)
    high = lax.axis_index("red") // 4
    swap = [(i, i ^ 1) for i in range(loops)]
    same_core = [[2 * i + c for i in range(chips)] for c in range(2)]
    rings = [[4 * h + x for x in range(4)] for h in range(2)]
    flip = [(i, (i + 4) % reds) for i in range(reds)]

    ids = query_ids.reshape(chips, 2, CHUNKS, -1).transpose(2, 1, 0, 3).reshape(queries)
    half = gradient.shape[1] // 2
    theirs = lax.dynamic_slice_in_dim(gradient, (1 - core) * half, half, 1)
    mine = lax.dynamic_slice_in_dim(gradient, core * half, half, 1)
    got = lax.ppermute(theirs, "loop", swap)
    sel = select(ids, out_basis)
    sel_got = lax.ppermute(sel, "loop", swap)

    eigen_rows = jnp.take(jnp.take(out_eigen, layer_index, axis=0)[0], ids)
    eigen_cols = jnp.take(in_eigen, layer_index, axis=0)[0]

    outs = []
    for n in range(CHUNKS):
        rows = slice(n * chunk, (n + 1) * chunk)
        part = pair_matmul(sel[rows], mine, sel_got[rows], got)
        part = lax.all_to_all(part.reshape(chips, -1, half), "loop", 0, 0, axis_index_groups=same_core)
        own = part.astype(F32).sum(0).astype(BF16)
        own = jnp.broadcast_to(own[None], (chips,) + own.shape)
        own = lax.all_to_all(own, "loop", 0, 0, axis_index_groups=same_core).reshape(chunk, half)
        other = lax.ppermute(own, "loop", swap)
        rot = rotate(core1, own, other, in_basis)
        rot = lax.all_to_all(rot.reshape(4, -1, rot.shape[1]), "red", 0, 0, axis_index_groups=rings)
        rot = rot.astype(F32).sum(0)
        piece = rot.shape[0] // 2
        send = lax.dynamic_slice_in_dim(rot, (1 - high) * piece, piece, 0).astype(BF16)
        keep = lax.dynamic_slice_in_dim(rot, high * piece, piece, 0)
        rot = keep + lax.ppermute(send, "red", flip).astype(F32)
        first = n * chunk + (lax.axis_index("red") % 4) * 2 * piece + high * piece
        er = lax.dynamic_slice_in_dim(eigen_rows, first, piece, 0)
        scaled = (rot / (er[:, None] * eigen_cols[None, :] + damping)).astype(BF16)
        far = lax.ppermute(scaled, "red", flip)
        scaled = jnp.where(high == 0, jnp.stack([scaled, far]), jnp.stack([far, scaled]))
        scaled = scaled.reshape(1, 2 * piece, -1)
        scaled = jnp.broadcast_to(scaled, (4,) + scaled.shape[1:])
        scaled = lax.all_to_all(scaled, "red", 0, 0, axis_index_groups=rings).reshape(chunk, -1)
        send, keep = back(core1, scaled, in_basis)
        total = (keep + lax.ppermute(send, "loop", swap).astype(F32)).astype(BF16)
        total = lax.all_to_all(total.reshape(chips, -1, total.shape[1]), "loop", 0, 0, axis_index_groups=same_core)
        outs.append(total.astype(F32).sum(0).astype(BF16))
    return jnp.concatenate(outs, 0)


def solution(mesh):
    return jax.shard_map(
        per_device,
        mesh=mesh,
        in_specs=(
            P(),
            P(),
            P("loop", "red"),
            P("loop", None),
            P("red", "loop"),
            P(),
            P(None, "loop"),
        ),
        out_specs=P("loop", "red"),
        check_vma=False,
    )
```

```python
import jax
import jax.numpy as jnp
from jax import lax
from jax.experimental import pallas as pl
from jax.experimental.pallas import tpu as pltpu
from jax.sharding import PartitionSpec as P

damping = 0.05
CHUNKS = 2
RING = 4
F32, BF16 = jnp.float32, jnp.bfloat16
NN = (((1,), (0,)), ((), ()))
NT = (((1,), (1,)), ((), ()))


def cost(flops, nbytes):
    return pl.CostEstimate(flops=flops, bytes_accessed=nbytes, transcendentals=0)


def dot(a, b, dims=NN):
    return lax.dot_general(a, b, dims, preferred_element_type=F32)


def params(mib):
    return pltpu.CompilerParams(vmem_limit_bytes=mib << 20)


def fixed(shape, at=(0, 0)):
    return pl.BlockSpec(shape, lambda *_: at)


def select_kernel(ids, basis, out, acc):
    step = pl.program_id(0)
    width = basis.shape[1]
    lanes = lax.broadcasted_iota(jnp.int32, (ids.shape[0], width), 1)
    hot = jnp.where(lanes == ids[...] - step * width, 1.0, 0.0).astype(BF16)
    part = dot(hot, basis[...], NT)

    @pl.when(step == 0)
    def _():
        acc[...] = part

    @pl.when(step > 0)
    def _():
        acc[...] += part

    @pl.when(step == pl.num_programs(0) - 1)
    def _():
        out[...] = acc[...].astype(BF16)


def select(ids, basis, block=1024):
    rows, width = basis.shape
    queries = ids.shape[0]
    return pl.pallas_call(
        select_kernel,
        grid=(width // block,),
        in_specs=[fixed((queries, 1)), pl.BlockSpec((rows, block), lambda i: (0, i))],
        out_specs=fixed((queries, rows)),
        out_shape=jax.ShapeDtypeStruct((queries, rows), BF16),
        scratch_shapes=[pltpu.VMEM((queries, rows), F32)],
        cost_estimate=cost(2 * queries * rows * width, rows * width * 2),
        compiler_params=params(56),
    )(ids[:, None], basis)


def rows_kernel(place, sel, grad, sel2, grad2, out):
    out[...] = (dot(sel[...], grad[...]) + dot(sel2[...], grad2[...])).astype(BF16)


def partial_rows(place, sel, grad, sel2, grad2, block=256):
    queries, units = sel.shape
    half = grad2.shape[1]
    steps = half // block
    return pl.pallas_call(
        rows_kernel,
        grid_spec=pltpu.PrefetchScalarGridSpec(
            num_scalar_prefetch=1,
            grid=(steps,),
            in_specs=[
                fixed((queries, units)),
                pl.BlockSpec((units, block), lambda i, place: (0, place[0] * steps + i)),
                fixed((queries, units)),
                pl.BlockSpec((units, block), lambda i, place: (0, i)),
            ],
            out_specs=pl.BlockSpec((queries, block), lambda i, place: (0, i)),
        ),
        out_shape=jax.ShapeDtypeStruct((queries, half), BF16),
        cost_estimate=cost(4 * queries * units * half, 6 * queries * half),
        compiler_params=params(32),
    )(place, sel, grad, sel2, grad2)


def rotate_kernel(place, own, other, basis, *refs):
    outs, lhs = refs[:RING], refs[RING]
    core, x = place[0], place[1]
    piece, half = outs[0].shape[0], own.shape[1]

    @pl.when(pl.program_id(0) == 0)
    def _():
        for d in range(RING):
            rows = pl.ds(pl.multiple_of(lax.rem(x + d, RING) * piece, piece), piece)
            to = pl.ds(d * piece, piece)
            lhs[core, to, :] = own[rows, :]
            lhs[1 - core, to, :] = other[rows, :]

    total = dot(lhs[0], basis[:half, :]) + dot(lhs[1], basis[half:, :])
    for d in range(RING):
        outs[d][...] = total[d * piece : (d + 1) * piece].astype(outs[d].dtype)


def rotate(place, own, other, basis, chunk_index, block=256):
    m, half = other.shape
    k, n = basis.shape
    piece = m // RING
    return pl.pallas_call(
        rotate_kernel,
        grid_spec=pltpu.PrefetchScalarGridSpec(
            num_scalar_prefetch=1,
            grid=(n // block,),
            in_specs=[
                fixed((m, half), (chunk_index, 0)),
                fixed((m, half)),
                pl.BlockSpec((k, block), lambda i, place: (0, i)),
            ],
            out_specs=[pl.BlockSpec((piece, block), lambda i, place: (0, i))] * RING,
            scratch_shapes=[pltpu.VMEM((2, m, half), BF16)],
        ),
        out_shape=[
            jax.ShapeDtypeStruct((piece, n), F32 if d == 0 else BF16) for d in range(RING)
        ],
        cost_estimate=cost(2 * m * k * n, 2 * (m * k + k * n + m * n)),
        compiler_params=params(50),
    )(place, own, other, basis)


def back_kernel(place, *refs):
    pieces, basis, other, own, lhs = refs[:RING], *refs[RING:]
    core, x = place[0], place[1]
    piece = pieces[0].shape[0]

    @pl.when(pl.program_id(0) == 0)
    def _():
        for d in range(RING):
            block = lax.rem(x + RING - d + 2 * (1 - core), RING)
            lhs[pl.ds(pl.multiple_of(block * piece, piece), piece), :] = pieces[d][...]

    total = dot(lhs[...], basis[...], NT)
    other[...] = total[: 2 * piece].astype(BF16)
    own[...] = total[2 * piece :]


def back(place, pieces, basis, block=512):
    piece, k = pieces[0].shape
    n = basis.shape[0]
    m = RING * piece
    return pl.pallas_call(
        back_kernel,
        grid_spec=pltpu.PrefetchScalarGridSpec(
            num_scalar_prefetch=1,
            grid=(n // block,),
            in_specs=[fixed((piece, k))] * RING
            + [pl.BlockSpec((block, k), lambda i, place: (i, 0))],
            out_specs=[pl.BlockSpec((m // 2, block), lambda i, place: (0, i))] * 2,
            scratch_shapes=[pltpu.VMEM((m, k), BF16)],
        ),
        out_shape=[
            jax.ShapeDtypeStruct((m // 2, n), BF16),
            jax.ShapeDtypeStruct((m // 2, n), F32),
        ],
        cost_estimate=cost(2 * m * k * n, 2 * (m * k + k * n + m * n)),
        compiler_params=params(50),
    )(place, *pieces, basis)


def ring_kernel(own, a, b, c, total, rounded):
    value = own[...] + a[...].astype(F32) + b[...].astype(F32) + c[...].astype(F32)
    total[...] = value
    rounded[...] = value.astype(BF16)


def ring_sum(parts):
    shape = parts[0].shape
    return pl.pallas_call(
        ring_kernel,
        in_specs=[pl.BlockSpec(memory_space=pltpu.VMEM)] * RING,
        out_specs=[pl.BlockSpec(memory_space=pltpu.VMEM)] * 2,
        out_shape=[jax.ShapeDtypeStruct(shape, F32), jax.ShapeDtypeStruct(shape, BF16)],
        cost_estimate=cost(3 * shape[0] * shape[1], 16 * shape[0] * shape[1]),
        compiler_params=params(8),
    )(*parts)


def scale_kernel(total, far, rows, cols, out):
    value = total[...] + far[...].astype(F32)
    out[...] = (value / (rows[...] * cols[...] + damping)).astype(BF16)


def scale(total, far, rows, cols):
    return pl.pallas_call(
        scale_kernel,
        in_specs=[pl.BlockSpec(memory_space=pltpu.VMEM)] * 4,
        out_specs=pl.BlockSpec(memory_space=pltpu.VMEM),
        out_shape=jax.ShapeDtypeStruct(total.shape, BF16),
        cost_estimate=cost(8 * total.size, 8 * total.size),
        compiler_params=params(8),
    )(total, far, rows, cols)


def add_up(parts):
    total = parts[0].astype(F32)
    for i in range(1, parts.shape[0]):
        total += parts[i].astype(F32)
    return total


def per_device(query_ids, layer_index, gradient, out_basis, in_basis, out_eigen, in_eigen):
    loops, reds = lax.axis_size("loop"), lax.axis_size("red")
    chips = loops // 2
    queries = query_ids.shape[0]
    chunk = queries // CHUNKS
    piece = chunk // RING
    core = lax.axis_index("loop") % 2
    x = lax.axis_index("red") % RING
    place = jnp.stack([core, x]).astype(jnp.int32)
    swap = [(i, i ^ 1) for i in range(loops)]
    flip = [(i, (i + RING) % reds) for i in range(reds)]
    shift = [[(i, i - i % RING + (i + d) % RING) for i in range(reds)] for d in range(RING)]
    same_core = [[2 * i + c for i in range(chips)] for c in range(2)]

    ids = query_ids.reshape(chips, 2, CHUNKS, -1).transpose(2, 1, 0, 3).reshape(queries)
    half = gradient.shape[1] // 2
    theirs = lax.dynamic_slice_in_dim(gradient, (1 - core) * half, half, 1)
    got = lax.ppermute(theirs, "loop", swap)
    sel = select(ids, out_basis)
    sel_got = lax.ppermute(sel, "loop", swap)
    part = partial_rows(place, sel, gradient, sel_got, got)
    part = lax.all_to_all(part.reshape(chips, -1, half), "loop", 0, 0, axis_index_groups=same_core)
    own = add_up(part).astype(BF16)
    own = jnp.broadcast_to(own[None], (chips,) + own.shape)
    own = lax.all_to_all(own, "loop", 0, 0, axis_index_groups=same_core).reshape(queries, half)

    eigen_rows = jnp.take(jnp.take(out_eigen, layer_index, axis=0)[0], ids)
    eigen_cols = jnp.take(in_eigen, layer_index, axis=0)[0]

    outs = []
    for n in range(CHUNKS):
        other = lax.ppermute(own[n * chunk : (n + 1) * chunk], "loop", swap)
        rot = rotate(place, own, other, in_basis, n)
        parts = [rot[0]] + [lax.ppermute(rot[d], "red", shift[d]) for d in range(1, RING)]
        total, rounded = ring_sum(parts)
        far = lax.ppermute(rounded, "red", flip)
        er = lax.dynamic_slice_in_dim(eigen_rows, n * chunk + x * piece, piece, 0)
        scaled = scale(total, far, er[:, None], eigen_cols[None, :])
        pieces = [scaled] + [lax.ppermute(scaled, "red", shift[d]) for d in range(1, RING)]
        send, keep = back(place, pieces, in_basis)
        total = (keep + lax.ppermute(send, "loop", swap).astype(F32)).astype(BF16)
        total = total.reshape(chips, -1, total.shape[1])
        total = lax.all_to_all(total, "loop", 0, 0, axis_index_groups=same_core)
        outs.append(add_up(total).astype(BF16))
    return jnp.concatenate(outs, 0)


def solution(mesh):
    return jax.shard_map(
        per_device,
        mesh=mesh,
        in_specs=(
            P(),
            P(),
            P("loop", "red"),
            P("loop", None),
            P("red", "loop"),
            P(),
            P(None, "loop"),
        ),
        out_specs=P("loop", "red"),
        check_vma=False,
    )
```

```python
import functools

import jax
import jax.numpy as jnp
from jax import lax
from jax.experimental import pallas as pl
from jax.experimental.pallas import tpu as pltpu
from jax.sharding import PartitionSpec as P

damping = 0.05
CHUNKS = 2
RING = 4
F32, BF16 = jnp.float32, jnp.bfloat16
VMEM = pl.BlockSpec(memory_space=pltpu.VMEM)
ANY = pl.BlockSpec(memory_space=pl.ANY)
SMEM = pl.BlockSpec(memory_space=pltpu.SMEM)
NN = (((1,), (0,)), ((), ()))
NT = (((1,), (1,)), ((), ()))


def cost(flops, nbytes):
    return pl.CostEstimate(flops=flops // 1000, bytes_accessed=nbytes // 1000, transcendentals=0)


def dot(a, b, dims=NN):
    return lax.dot_general(a, b, dims, preferred_element_type=F32)


def params(mib):
    return pltpu.CompilerParams(vmem_limit_bytes=mib << 20)


def fixed(shape, at=(0, 0)):
    return pl.BlockSpec(shape, lambda *_: at)


def select_kernel(ids, basis, out, acc, *, chips):
    step = pl.program_id(0)
    width, queries = basis.shape[1], ids.shape[1]
    want = (ids[...] - step * width).astype(jnp.int16)
    lanes = lax.broadcasted_iota(jnp.int16, (width, queries), 0)
    hot = jnp.where(lanes == want, jnp.ones((), BF16), jnp.zeros((), BF16))
    part = dot(basis[...], hot)

    @pl.when(step == 0)
    def _():
        acc[...] = part

    @pl.when(step > 0)
    def _():
        acc[...] += part

    @pl.when(step == pl.num_programs(0) - 1)
    def _():
        rows = acc[...].T.astype(BF16)
        share = queries // chips // CHUNKS
        run = share // 2
        for chip in range(chips):
            for core in range(2):
                for n in range(CHUNKS):
                    at = (core * chips + chip) * run
                    to = at // share * (share * CHUNKS) + n * share + at % share
                    at = ((chip * 2 + core) * CHUNKS + n) * run
                    out[to : to + run, :] = rows[at : at + run, :]


def select(ids, basis, chips, block=2048):
    rows, width = basis.shape
    queries = ids.shape[0]
    return pl.pallas_call(
        functools.partial(select_kernel, chips=chips),
        grid=(width // block,),
        in_specs=[fixed((1, queries)), pl.BlockSpec((rows, block), lambda i: (0, i))],
        out_specs=fixed((queries, rows)),
        out_shape=jax.ShapeDtypeStruct((queries, rows), BF16),
        scratch_shapes=[pltpu.VMEM((rows, queries), F32)],
        cost_estimate=cost(2 * queries * rows * width, rows * width * 2),
        compiler_params=params(56),
    )(ids[None, :], basis)


def rows_kernel(place, sel, sel2, grad, grad2, out, buf, buf2, sems):
    steps = sems.shape[1]
    half = out.shape[1]
    block = half // steps
    copies = []
    for i in range(steps):
        at = pl.ds(pl.multiple_of(place[0] * half + i * block, block), block)
        to = pl.ds(i * block, block)
        copies.append(
            [
                pltpu.make_async_copy(grad.at[:, at], buf.at[:, to], sems.at[0, i]),
                pltpu.make_async_copy(grad2.at[:, at], buf2.at[:, to], sems.at[1, i]),
            ]
        )
    for first, second in copies:
        first.start()
        second.start()
    for i in range(steps):
        to = pl.ds(i * block, block)
        copies[i][0].wait()
        copies[i][1].wait()
        total = dot(sel[...], buf[:, to]) + dot(sel2[...], buf2[:, to])
        out[:, to] = total.astype(BF16)


def partial_rows(place, sel, sel2, grad, grad2, steps=2):
    queries, units = sel.shape
    half = grad.shape[1] // 2
    return pl.pallas_call(
        rows_kernel,
        in_specs=[SMEM, VMEM, VMEM, ANY, ANY],
        out_specs=VMEM,
        out_shape=jax.ShapeDtypeStruct((queries, half), BF16),
        scratch_shapes=[
            pltpu.VMEM((units, half), BF16),
            pltpu.VMEM((units, half), BF16),
            pltpu.SemaphoreType.DMA((2, steps)),
        ],
        cost_estimate=cost(4 * queries * units * half, 6 * queries * half),
        compiler_params=params(56),
    )(place, sel, sel2, grad, grad2)


def fetch(basis, buf, sems, cuts):
    copies = []
    for i, (start, size) in enumerate(cuts):
        at = pl.ds(start, size)
        copies.append(pltpu.make_async_copy(basis.at[at, :], buf.at[at, :], sems.at[i]))
    for copy in copies:
        copy.start()
    return copies


def rotate_kernel(place, own, other, basis, *refs, cuts):
    outs, (lhs, buf, acc, sems) = refs[:RING], refs[RING:]
    copies = fetch(basis, buf, sems, cuts)
    core, x = place[0], place[1]
    piece, half = outs[0].shape[0], own.shape[1]
    for d in range(RING):
        rows = pl.ds(pl.multiple_of(lax.rem(x + d, RING) * piece, piece), piece)
        to = pl.ds(d * piece, piece)
        lhs[core, to, :] = own[rows, :]
        lhs[1 - core, to, :] = other[rows, :]
    for i, (start, size) in enumerate(cuts):
        copies[i].wait()
        part = lhs[start // half, :, start % half : start % half + size]
        value = dot(part, buf[start : start + size, :])
        if i > 0:
            value += acc[...]
        if i < len(cuts) - 1:
            acc[...] = value
        else:
            for d in range(RING):
                outs[d][...] = value[d * piece : (d + 1) * piece].astype(outs[d].dtype)


def rotate(place, own, other, basis):
    m, half = other.shape
    k, n = basis.shape
    piece = m // RING
    block = half // 7
    cuts = [(h * half + at * block, size * block) for h in range(2) for at, size in ((0, 3), (3, 2), (5, 2))]
    return pl.pallas_call(
        functools.partial(rotate_kernel, cuts=cuts),
        in_specs=[SMEM, VMEM, VMEM, ANY],
        out_specs=[VMEM] * RING,
        out_shape=[
            jax.ShapeDtypeStruct((piece, n), F32 if d == 0 else BF16) for d in range(RING)
        ],
        scratch_shapes=[
            pltpu.VMEM((2, m, half), BF16),
            pltpu.VMEM((k, n), BF16),
            pltpu.VMEM((m, n), F32),
            pltpu.SemaphoreType.DMA((len(cuts),)),
        ],
        cost_estimate=cost(2 * m * k * n, 2 * k * n),
        compiler_params=params(50),
    )(place, own, other, basis)


def back_kernel(place, *refs, cuts):
    pieces, (basis, other, own, lhs, rhs, buf, sems) = refs[:RING], refs[RING:]
    copies = fetch(basis, buf, sems, cuts)
    core, x = place[0], place[1]
    piece = pieces[0].shape[0]
    for d in range(RING):
        to = lax.rem(x + RING - d + 2 * (1 - core), RING)
        lhs[pl.ds(pl.multiple_of(to * piece, piece), piece), :] = pieces[d][...]
    rhs[...] = lhs[...].T
    for i, (start, size) in enumerate(cuts):
        copies[i].wait()
        total = dot(buf[start : start + size, :], rhs[...]).T
        other[:, start : start + size] = total[: 2 * piece].astype(BF16)
        own[:, start : start + size] = total[2 * piece :]


def back(place, pieces, basis):
    piece, k = pieces[0].shape
    n = basis.shape[0]
    m = RING * piece
    cuts = [(i * n // 7, n // 7) for i in range(7)]
    return pl.pallas_call(
        functools.partial(back_kernel, cuts=cuts),
        in_specs=[SMEM] + [VMEM] * RING + [ANY],
        out_specs=[VMEM] * 2,
        out_shape=[
            jax.ShapeDtypeStruct((m // 2, n), BF16),
            jax.ShapeDtypeStruct((m // 2, n), F32),
        ],
        scratch_shapes=[
            pltpu.VMEM((m, k), BF16),
            pltpu.VMEM((k, m), BF16),
            pltpu.VMEM((n, k), BF16),
            pltpu.SemaphoreType.DMA((len(cuts),)),
        ],
        cost_estimate=cost(2 * m * k * n, 2 * k * n),
        compiler_params=params(50),
    )(place, *pieces, basis)


def ring_kernel(own, a, b, c, total, rounded):
    value = own[...] + a[...].astype(F32) + b[...].astype(F32) + c[...].astype(F32)
    total[...] = value
    rounded[...] = value.astype(BF16)


def ring_sum(parts):
    shape = parts[0].shape
    return pl.pallas_call(
        ring_kernel,
        in_specs=[VMEM] * RING,
        out_specs=[VMEM] * 2,
        out_shape=[jax.ShapeDtypeStruct(shape, F32), jax.ShapeDtypeStruct(shape, BF16)],
        cost_estimate=cost(3 * shape[0] * shape[1], 16 * shape[0] * shape[1]),
        compiler_params=params(8),
    )(*parts)


def scale_kernel(total, far, rows, cols, out):
    value = total[...] + far[...].astype(F32)
    out[...] = (value / (rows[...] * cols[...] + damping)).astype(BF16)


def scale(total, far, rows, cols):
    return pl.pallas_call(
        scale_kernel,
        in_specs=[VMEM] * 4,
        out_specs=VMEM,
        out_shape=jax.ShapeDtypeStruct(total.shape, BF16),
        cost_estimate=cost(8 * total.size, 8 * total.size),
        compiler_params=params(8),
    )(total, far, rows, cols)


def add_up(parts):
    total = parts[0].astype(F32)
    for i in range(1, parts.shape[0]):
        total += parts[i].astype(F32)
    return total


def tie(*values):
    return lax.optimization_barrier(values)


def per_device(query_ids, layer_index, gradient, out_basis, in_basis, out_eigen, in_eigen):
    loops, reds = lax.axis_size("loop"), lax.axis_size("red")
    chips = loops // 2
    queries = query_ids.shape[0]
    chunk = queries // CHUNKS
    piece = chunk // RING
    core = lax.axis_index("loop") % 2
    x = lax.axis_index("red") % RING
    place = jnp.stack([core, x]).astype(jnp.int32)
    swap = [(i, i ^ 1) for i in range(loops)]
    flip = [(i, (i + RING) % reds) for i in range(reds)]
    shift = [[(i, i - i % RING + (i + d) % RING) for i in range(reds)] for d in range(RING)]
    same_core = [[2 * i + c for i in range(chips)] for c in range(2)]

    def exchange(value):
        value = value.reshape(chips, -1, value.shape[1])
        return lax.all_to_all(value, "loop", 0, 0, axis_index_groups=same_core)

    got = lax.ppermute(gradient, "loop", swap)
    sel = select(query_ids, out_basis, chips)
    sel_got = lax.ppermute(sel, "loop", swap)
    part = partial_rows(place, sel, sel_got, gradient, got)
    part = exchange(part)
    eigen_rows = jnp.take(jnp.take(out_eigen, layer_index, axis=0)[0], query_ids)
    eigen_rows = eigen_rows.reshape(chips, 2, CHUNKS, -1).transpose(2, 1, 0, 3).reshape(CHUNKS, chunk)
    eigen_cols = jnp.take(in_eigen, layer_index, axis=0)
    factors = [
        lax.dynamic_slice_in_dim(eigen_rows[n], x * piece, piece, 0)[:, None] for n in range(CHUNKS)
    ]
    rows_w, *factors = tie(add_up(part).astype(BF16), *factors)
    share = rows_w.shape[0] // CHUNKS

    def gather(rows):
        rows = jnp.broadcast_to(rows[None], (chips,) + rows.shape).reshape(chunk, -1)
        return exchange(rows).reshape(chunk, -1)

    def ring(parts):
        return [parts[0]] + [lax.ppermute(parts[d], "red", shift[d]) for d in range(1, RING)]

    def swapped(value):
        return lax.ppermute(value, "loop", swap)

    own_a = gather(rows_w[:share])
    rows_b, own_a = tie(rows_w[share:], own_a)
    own_b = gather(rows_b)
    rot_a = rotate(place, own_a, swapped(own_a), in_basis)
    ring_a = ring(rot_a)
    own_b, *ring_a = tie(own_b, *ring_a)
    other_b = swapped(own_b)
    total_a, rounded_a = ring_sum(ring_a)
    other_b, total_a = tie(other_b, total_a)
    rot_b = rotate(place, own_b, other_b, in_basis)
    scaled_a = scale(total_a, lax.ppermute(rounded_a, "red", flip), factors[0], eigen_cols)
    ring_b = ring(rot_b)
    pieces_a = ring([scaled_a] * RING)
    total_b, rounded_b = ring_sum(ring_b)
    pieces_a[0], total_b = tie(pieces_a[0], total_b)
    send_a, keep_a = back(place, pieces_a, in_basis)
    scaled_b = scale(total_b, lax.ppermute(rounded_b, "red", flip), factors[1], eigen_cols)
    pieces_b = ring([scaled_b] * RING)
    part_a = (keep_a + swapped(send_a).astype(F32)).astype(BF16)
    pieces_b[0], part_a = tie(pieces_b[0], part_a)
    part_a = exchange(part_a)
    part_a, *pieces_b = tie(part_a, *pieces_b)
    send_b, keep_b = back(place, pieces_b, in_basis)
    part_b = exchange((keep_b + swapped(send_b).astype(F32)).astype(BF16))
    return jnp.concatenate([add_up(part_a).astype(BF16), add_up(part_b).astype(BF16)], 0)


def solution(mesh):
    return jax.shard_map(
        per_device,
        mesh=mesh,
        in_specs=(
            P(),
            P(),
            P("loop", "red"),
            P("loop", None),
            P("red", "loop"),
            P(),
            P(None, "loop"),
        ),
        out_specs=P("loop", "red"),
        check_vma=False,
    )
```

```python
import functools

import jax
import jax.numpy as jnp
from jax import lax
from jax.experimental import pallas as pl
from jax.experimental.pallas import tpu as pltpu
from jax.sharding import PartitionSpec as P

damping = 0.05
CHUNKS = 1
RING = 4
F32, BF16 = jnp.float32, jnp.bfloat16
VMEM = pl.BlockSpec(memory_space=pltpu.VMEM)
ANY = pl.BlockSpec(memory_space=pl.ANY)
SMEM = pl.BlockSpec(memory_space=pltpu.SMEM)
NN = (((1,), (0,)), ((), ()))
NT = (((1,), (1,)), ((), ()))


def cost(flops, nbytes):
    return pl.CostEstimate(flops=flops // 1000, bytes_accessed=nbytes // 1000, transcendentals=0)


def dot(a, b, dims=NN):
    return lax.dot_general(a, b, dims, preferred_element_type=F32)


def params(mib):
    return pltpu.CompilerParams(vmem_limit_bytes=mib << 20)


def fixed(shape, at=(0, 0)):
    return pl.BlockSpec(shape, lambda *_: at)


def select_kernel(ids, basis, out, acc, *, chips):
    step = pl.program_id(0)
    width, queries = basis.shape[1], ids.shape[1]
    want = (ids[...] - step * width).astype(jnp.int16)
    lanes = lax.broadcasted_iota(jnp.int16, (width, queries), 0)
    hot = jnp.where(lanes == want, jnp.ones((), BF16), jnp.zeros((), BF16))
    part = dot(basis[...], hot)

    @pl.when(step == 0)
    def _():
        acc[...] = part

    @pl.when(step > 0)
    def _():
        acc[...] += part

    @pl.when(step == pl.num_programs(0) - 1)
    def _():
        rows = acc[...].T.astype(BF16)
        share = queries // chips // CHUNKS
        run = share // 2
        for chip in range(chips):
            for core in range(2):
                for n in range(CHUNKS):
                    at = (core * chips + chip) * run
                    to = at // share * (share * CHUNKS) + n * share + at % share
                    at = ((chip * 2 + core) * CHUNKS + n) * run
                    out[to : to + run, :] = rows[at : at + run, :]


def select(ids, basis, chips, block=2048):
    rows, width = basis.shape
    queries = ids.shape[0]
    return pl.pallas_call(
        functools.partial(select_kernel, chips=chips),
        grid=(width // block,),
        in_specs=[fixed((1, queries)), pl.BlockSpec((rows, block), lambda i: (0, i))],
        out_specs=fixed((queries, rows)),
        out_shape=jax.ShapeDtypeStruct((queries, rows), BF16),
        scratch_shapes=[pltpu.VMEM((rows, queries), F32)],
        cost_estimate=cost(2 * queries * rows * width, rows * width * 2),
        compiler_params=params(56),
    )(ids[None, :], basis)


def fetch(source, buf, sems, cuts):
    copies = []
    for i, (at, to) in enumerate(cuts):
        copies.append(pltpu.make_async_copy(source.at[at], buf.at[to], sems.at[i]))
    for copy in copies:
        copy.start()
    return copies


def rows_kernel(place, sel, grad, *refs):
    before, (out, buf, sems) = refs[:-3], refs[-3:]
    half = out.shape[1]
    block = half // sems.shape[0]
    cuts = []
    for i in range(sems.shape[0]):
        at = pl.ds(pl.multiple_of(place[0] * half + i * block, block), block)
        cuts.append(((slice(None), at), (slice(None), pl.ds(i * block, block))))
    copies = fetch(grad, buf, sems, cuts)
    for i in range(sems.shape[0]):
        to = pl.ds(i * block, block)
        copies[i].wait()
        total = dot(sel[...], buf[:, to])
        for ref in before:
            total += ref[:, to]
        out[:, to] = total.astype(out.dtype)


def partial_rows(place, sel, grad, *before, steps=2):
    queries, units = sel.shape
    half = grad.shape[1] // 2
    return pl.pallas_call(
        rows_kernel,
        in_specs=[SMEM, VMEM, ANY] + [VMEM] * len(before),
        out_specs=VMEM,
        out_shape=jax.ShapeDtypeStruct((queries, half), BF16 if before else F32),
        scratch_shapes=[pltpu.VMEM((units, half), BF16), pltpu.SemaphoreType.DMA((steps,))],
        cost_estimate=cost(2 * queries * units * half, 6 * queries * half),
        compiler_params=params(56),
    )(place, sel, grad, *before)


def rotate_own_kernel(place, own, basis, acc, lhs, buf, sems):
    core, x = place[0], place[1]
    half, steps = own.shape[1], sems.shape[0]
    block = basis.shape[1] // steps
    at = pl.ds(pl.multiple_of(core * half, half), half)
    blocks = [pl.ds(i * block, block) for i in range(steps)]
    copies = fetch(basis, buf, sems, [((at, to), (slice(None), to)) for to in blocks])
    piece = own.shape[0] // RING
    for d in range(RING):
        rows = pl.ds(pl.multiple_of(lax.rem(x + d, RING) * piece, piece), piece)
        lhs[d * piece : (d + 1) * piece, :] = own[rows, :]
    for i in range(steps):
        copies[i].wait()
        acc[:, blocks[i]] = dot(lhs[...], buf[:, blocks[i]])


def rotate_other_kernel(place, other, basis, acc, *refs):
    outs, (lhs, buf, sems) = refs[:RING], refs[RING:]
    core, x = place[0], place[1]
    half, steps = other.shape[1], sems.shape[0]
    block = basis.shape[1] // steps
    at = pl.ds(pl.multiple_of((1 - core) * half, half), half)
    blocks = [pl.ds(i * block, block) for i in range(steps)]
    copies = fetch(basis, buf, sems, [((at, to), (slice(None), to)) for to in blocks])
    piece = other.shape[0] // RING
    for d in range(RING):
        rows = pl.ds(pl.multiple_of(lax.rem(x + d, RING) * piece, piece), piece)
        lhs[d * piece : (d + 1) * piece, :] = other[rows, :]
    for i in range(steps):
        copies[i].wait()
        total = dot(lhs[...], buf[:, blocks[i]]) + acc[:, blocks[i]]
        for d in range(RING):
            outs[d][:, blocks[i]] = total[d * piece : (d + 1) * piece].astype(outs[d].dtype)


def rotate(place, rows, basis, acc=None, steps=2):
    m, half = rows.shape
    n = basis.shape[1]
    scratch = [
        pltpu.VMEM((m, half), BF16),
        pltpu.VMEM((half, n), BF16),
        pltpu.SemaphoreType.DMA((steps,)),
    ]
    if acc is None:
        return pl.pallas_call(
            rotate_own_kernel,
            in_specs=[SMEM, VMEM, ANY],
            out_specs=VMEM,
            out_shape=jax.ShapeDtypeStruct((m, n), F32),
            scratch_shapes=scratch,
            cost_estimate=cost(2 * m * half * n, 2 * half * n),
            compiler_params=params(52),
        )(place, rows, basis)
    return pl.pallas_call(
        rotate_other_kernel,
        in_specs=[SMEM, VMEM, ANY, VMEM],
        out_specs=[VMEM] * RING,
        out_shape=[
            jax.ShapeDtypeStruct((m // RING, n), F32 if d == 0 else BF16) for d in range(RING)
        ],
        scratch_shapes=scratch,
        cost_estimate=cost(2 * m * half * n, 2 * half * n),
        compiler_params=params(52),
    )(place, rows, basis, acc)


def back_kernel(place, *refs):
    pieces, (basis, other, own, lhs, rhs, buf, sems) = refs[:RING], refs[RING:]
    block = basis.shape[0] // sems.shape[0]
    blocks = [pl.ds(i * block, block) for i in range(sems.shape[0])]
    copies = fetch(basis, buf, sems, [((at,), (at,)) for at in blocks])
    core, x = place[0], place[1]
    piece = pieces[0].shape[0]
    for d in range(RING):
        to = lax.rem(x + RING - d + 2 * (1 - core), RING)
        lhs[pl.ds(pl.multiple_of(to * piece, piece), piece), :] = pieces[d][...]
    rhs[...] = lhs[...].T
    for i, at in enumerate(blocks):
        copies[i].wait()
        total = dot(buf[at, :], rhs[...]).T
        other[:, at] = total[: 2 * piece].astype(BF16)
        own[:, at] = total[2 * piece :]


def back(place, pieces, basis, steps=7):
    piece, k = pieces[0].shape
    n = basis.shape[0]
    m = RING * piece
    return pl.pallas_call(
        back_kernel,
        in_specs=[SMEM] + [VMEM] * RING + [ANY],
        out_specs=[VMEM] * 2,
        out_shape=[
            jax.ShapeDtypeStruct((m // 2, n), BF16),
            jax.ShapeDtypeStruct((m // 2, n), F32),
        ],
        scratch_shapes=[
            pltpu.VMEM((m, k), BF16),
            pltpu.VMEM((k, m), BF16),
            pltpu.VMEM((n, k), BF16),
            pltpu.SemaphoreType.DMA((steps,)),
        ],
        cost_estimate=cost(2 * m * k * n, 2 * k * n),
        compiler_params=params(52),
    )(place, *pieces, basis)


def ring_kernel(own, a, b, c, total, rounded):
    value = own[...] + a[...].astype(F32) + b[...].astype(F32) + c[...].astype(F32)
    total[...] = value
    rounded[...] = value.astype(BF16)


def ring_sum(parts):
    shape = parts[0].shape
    return pl.pallas_call(
        ring_kernel,
        in_specs=[VMEM] * RING,
        out_specs=[VMEM] * 2,
        out_shape=[jax.ShapeDtypeStruct(shape, F32), jax.ShapeDtypeStruct(shape, BF16)],
        cost_estimate=cost(3 * shape[0] * shape[1], 16 * shape[0] * shape[1]),
        compiler_params=params(16),
    )(*parts)


def scale_kernel(total, far, rows, cols, out):
    value = total[...] + far[...].astype(F32)
    out[...] = (value / (rows[...] * cols[...] + damping)).astype(BF16)


def scale(total, far, rows, cols):
    return pl.pallas_call(
        scale_kernel,
        in_specs=[VMEM] * 4,
        out_specs=VMEM,
        out_shape=jax.ShapeDtypeStruct(total.shape, BF16),
        cost_estimate=cost(8 * total.size, 8 * total.size),
        compiler_params=params(16),
    )(total, far, rows, cols)


def add_up(parts):
    total = parts[0].astype(F32)
    for i in range(1, parts.shape[0]):
        total += parts[i].astype(F32)
    return total


def tie(*values):
    return lax.optimization_barrier(values)


def per_device(query_ids, layer_index, gradient, out_basis, in_basis, out_eigen, in_eigen):
    loops, reds = lax.axis_size("loop"), lax.axis_size("red")
    chips = loops // 2
    queries = query_ids.shape[0]
    chunk = queries // CHUNKS
    piece = chunk // RING
    core = lax.axis_index("loop") % 2
    x = lax.axis_index("red") % RING
    place = jnp.stack([core, x]).astype(jnp.int32)
    half = gradient.shape[1] // 2
    swap = [(i, i ^ 1) for i in range(loops)]
    flip = [(i, (i + RING) % reds) for i in range(reds)]
    shift = [[(i, i - i % RING + (i + d) % RING) for i in range(reds)] for d in range(RING)]
    same_core = [[2 * i + c for i in range(chips)] for c in range(2)]

    def exchange(value):
        value = value.reshape(chips, -1, value.shape[1])
        return lax.all_to_all(value, "loop", 0, 0, axis_index_groups=same_core)

    got = lax.ppermute(gradient, "loop", swap)
    sel = select(query_ids, out_basis, chips)
    sel_got = lax.ppermute(sel, "loop", swap)
    part = partial_rows(place, sel, gradient)
    part = exchange(partial_rows(place, sel_got, got, part))
    eigen_rows = jnp.take(jnp.take(out_eigen, layer_index, axis=0)[0], query_ids)
    eigen_rows = eigen_rows.reshape(chips, 2, -1).transpose(1, 0, 2).reshape(queries)
    eigen_rows = lax.dynamic_slice_in_dim(eigen_rows, x * piece, piece, 0)[:, None]
    eigen_cols = jnp.take(in_eigen, layer_index, axis=0)
    rows_w, eigen_rows = tie(add_up(part).astype(BF16), eigen_rows)

    def ring(parts):
        return [parts[0]] + [lax.ppermute(parts[d], "red", shift[d]) for d in range(1, RING)]

    own = jnp.broadcast_to(rows_w[None], (chips,) + rows_w.shape).reshape(queries, half)
    own = exchange(own).reshape(queries, half)
    other = lax.ppermute(own, "loop", swap)
    rot = rotate(place, other, in_basis, rotate(place, own, in_basis))
    total, rounded = ring_sum(ring(rot))
    scaled = scale(total, lax.ppermute(rounded, "red", flip), eigen_rows, eigen_cols)
    send, keep = back(place, ring([scaled] * RING), in_basis)
    part = exchange((keep + lax.ppermute(send, "loop", swap).astype(F32)).astype(BF16))
    return add_up(part).astype(BF16)


def solution(mesh):
    return jax.shard_map(
        per_device,
        mesh=mesh,
        in_specs=(
            P(),
            P(),
            P("loop", "red"),
            P("loop", None),
            P("red", "loop"),
            P(),
            P(None, "loop"),
        ),
        out_specs=P("loop", "red"),
        check_vma=False,
    )
```

```python
import functools

import jax
import jax.numpy as jnp
from jax import lax
from jax.experimental import pallas as pl
from jax.experimental.pallas import tpu as pltpu
from jax.sharding import PartitionSpec as P

damping = 0.05
CHUNKS = 2
RING = 4
F32, BF16 = jnp.float32, jnp.bfloat16
VMEM = pl.BlockSpec(memory_space=pltpu.VMEM)
ANY = pl.BlockSpec(memory_space=pl.ANY)
SMEM = pl.BlockSpec(memory_space=pltpu.SMEM)
NN = (((1,), (0,)), ((), ()))
NT = (((1,), (1,)), ((), ()))


def cost(flops, nbytes):
    return pl.CostEstimate(flops=flops, bytes_accessed=nbytes, transcendentals=0)


def dot(a, b, dims=NN):
    return lax.dot_general(a, b, dims, preferred_element_type=F32)


def params(mib):
    return pltpu.CompilerParams(vmem_limit_bytes=mib << 20)


def fixed(shape, at=(0, 0)):
    return pl.BlockSpec(shape, lambda *_: at)


def select_kernel(ids, basis, out, acc, *, chips):
    step = pl.program_id(0)
    width, queries = basis.shape[1], ids.shape[1]
    want = (ids[...] - step * width).astype(jnp.int16)
    lanes = lax.broadcasted_iota(jnp.int16, (width, queries), 0)
    hot = jnp.where(lanes == want, jnp.ones((), BF16), jnp.zeros((), BF16))
    part = dot(basis[...], hot)

    @pl.when(step == 0)
    def _():
        acc[...] = part

    @pl.when(step > 0)
    def _():
        acc[...] += part

    @pl.when(step == pl.num_programs(0) - 1)
    def _():
        rows = acc[...].T.astype(BF16)
        share = queries // chips // CHUNKS
        run = share // 2
        for chip in range(chips):
            for core in range(2):
                for n in range(CHUNKS):
                    at = (core * chips + chip) * run
                    to = at // share * (share * CHUNKS) + n * share + at % share
                    at = ((chip * 2 + core) * CHUNKS + n) * run
                    out[to : to + run, :] = rows[at : at + run, :]


def select(ids, basis, chips, block=2048):
    rows, width = basis.shape
    queries = ids.shape[0]
    return pl.pallas_call(
        functools.partial(select_kernel, chips=chips),
        grid=(width // block,),
        in_specs=[fixed((1, queries)), pl.BlockSpec((rows, block), lambda i: (0, i))],
        out_specs=fixed((queries, rows)),
        out_shape=jax.ShapeDtypeStruct((queries, rows), BF16),
        scratch_shapes=[pltpu.VMEM((rows, queries), F32)],
        cost_estimate=cost(2 * queries * rows * width, rows * width * 2),
        compiler_params=params(56),
    )(ids[None, :], basis)


def rows_kernel(place, sel, sel2, grad, grad2, out, buf, buf2, sems):
    steps = sems.shape[1]
    half = out.shape[1]
    block = half // steps
    copies = []
    for i in range(steps):
        at = pl.ds(pl.multiple_of(place[0] * half + i * block, block), block)
        to = pl.ds(i * block, block)
        copies.append(
            [
                pltpu.make_async_copy(grad.at[:, at], buf.at[:, to], sems.at[0, i]),
                pltpu.make_async_copy(grad2.at[:, at], buf2.at[:, to], sems.at[1, i]),
            ]
        )
    for first, second in copies:
        first.start()
        second.start()
    for i in range(steps):
        to = pl.ds(i * block, block)
        copies[i][0].wait()
        copies[i][1].wait()
        total = dot(sel[...], buf[:, to]) + dot(sel2[...], buf2[:, to])
        out[:, to] = total.astype(BF16)


def partial_rows(place, sel, sel2, grad, grad2, steps=2):
    queries, units = sel.shape
    half = grad.shape[1] // 2
    return pl.pallas_call(
        rows_kernel,
        in_specs=[SMEM, VMEM, VMEM, ANY, ANY],
        out_specs=VMEM,
        out_shape=jax.ShapeDtypeStruct((queries, half), BF16),
        scratch_shapes=[
            pltpu.VMEM((units, half), BF16),
            pltpu.VMEM((units, half), BF16),
            pltpu.SemaphoreType.DMA((2, steps)),
        ],
        cost_estimate=cost(4 * queries * units * half, 6 * queries * half),
        compiler_params=params(56),
    )(place, sel, sel2, grad, grad2)


def fetch(basis, buf, sems, cuts):
    copies = []
    for i, (start, size) in enumerate(cuts):
        at = pl.ds(start, size)
        copies.append(pltpu.make_async_copy(basis.at[at, :], buf.at[at, :], sems.at[i]))
    for copy in copies:
        copy.start()
    return copies


def rotate_kernel(place, own, other, basis, *refs, cuts):
    outs, (lhs, buf, acc, sems) = refs[:-4], refs[-4:]
    copies = fetch(basis, buf, sems, cuts)
    core, x = place[0], place[1] if len(outs) > 1 else 0
    piece, half = own.shape[0] // RING, own.shape[1]
    for d in range(RING):
        rows = pl.ds(pl.multiple_of(lax.rem(x + d, RING) * piece, piece), piece)
        to = pl.ds(d * piece, piece)
        lhs[core, to, :] = own[rows, :]
        lhs[1 - core, to, :] = other[rows, :]
    for i, (start, size) in enumerate(cuts):
        copies[i].wait()
        part = lhs[start // half, :, start % half : start % half + size]
        value = dot(part, buf[start : start + size, :])
        if i > 0:
            value += acc[...]
        if i < len(cuts) - 1:
            acc[...] = value
        elif len(outs) == 1:
            outs[0][...] = value.astype(BF16)
        else:
            for d in range(RING):
                outs[d][...] = value[d * piece : (d + 1) * piece].astype(outs[d].dtype)


def rotate(place, own, other, basis, stacked=False):
    m, half = other.shape
    k, n = basis.shape
    piece = m // RING
    outs = [jax.ShapeDtypeStruct((piece, n), F32 if d == 0 else BF16) for d in range(RING)]
    if stacked:
        outs = [jax.ShapeDtypeStruct((m, n), BF16)]
    block = half // 7
    cuts = [(h * half + at * block, size * block) for h in range(2) for at, size in ((0, 3), (3, 2), (5, 2))]
    return pl.pallas_call(
        functools.partial(rotate_kernel, cuts=cuts),
        in_specs=[SMEM, VMEM, VMEM, ANY],
        out_specs=[VMEM] * len(outs),
        out_shape=outs,
        scratch_shapes=[
            pltpu.VMEM((2, m, half), BF16),
            pltpu.VMEM((k, n), BF16),
            pltpu.VMEM((m, n), F32),
            pltpu.SemaphoreType.DMA((len(cuts),)),
        ],
        cost_estimate=cost(2 * m * k * n, 2 * k * n),
        compiler_params=params(50),
    )(place, own, other, basis)


def back_kernel(place, *refs, cuts):
    pieces, (basis, other, own, lhs, buf, send, keep, sems, out_sems) = refs[:RING], refs[RING:]
    copies = fetch(basis, buf, sems, cuts)
    core, x = place[0], place[1]
    piece = pieces[0].shape[0]
    for d in range(RING):
        to = lax.rem(x + RING - d + 2 * (1 - core), RING)
        lhs[pl.ds(pl.multiple_of(to * piece, piece), piece), :] = pieces[d][...]
    stores = []
    for i, (start, size) in enumerate(cuts):
        at = pl.ds(start, size)
        copies[i].wait()
        total = dot(lhs[...], buf[at, :], NT)
        send[:, at] = total[: 2 * piece].astype(BF16)
        keep[:, at] = total[2 * piece :]
        stores.append(pltpu.make_async_copy(send.at[:, at], other.at[:, at], out_sems.at[0, i]))
        stores[-1].start()
        stores.append(pltpu.make_async_copy(keep.at[:, at], own.at[:, at], out_sems.at[1, i]))
        stores[-1].start()
    for store in stores:
        store.wait()


def back(place, pieces, basis):
    piece, k = pieces[0].shape
    n = basis.shape[0]
    m = RING * piece
    cuts = [(i * n // 7, n // 7) for i in range(7)]
    return pl.pallas_call(
        functools.partial(back_kernel, cuts=cuts),
        in_specs=[SMEM] + [VMEM] * RING + [ANY],
        out_specs=[ANY] * 2,
        out_shape=[
            jax.ShapeDtypeStruct((m // 2, n), BF16),
            jax.ShapeDtypeStruct((m // 2, n), F32),
        ],
        scratch_shapes=[
            pltpu.VMEM((m, k), BF16),
            pltpu.VMEM((n, k), BF16),
            pltpu.VMEM((m // 2, n), BF16),
            pltpu.VMEM((m // 2, n), F32),
            pltpu.SemaphoreType.DMA((len(cuts),)),
            pltpu.SemaphoreType.DMA((2, len(cuts))),
        ],
        cost_estimate=cost(2 * m * k * n, 2 * k * n),
        compiler_params=params(50),
    )(place, *pieces, basis)


def join_kernel(keep, got, out):
    out[...] = (keep[...] + got[...].astype(F32)).astype(BF16)


def join(keep, got):
    return pl.pallas_call(
        join_kernel,
        in_specs=[VMEM] * 2,
        out_specs=VMEM,
        out_shape=jax.ShapeDtypeStruct(got.shape, BF16),
        cost_estimate=cost(2 * got.size, 8 * got.size),
        compiler_params=params(8),
    )(keep, got)


def stack_kernel(parts, total, rounded):
    value = parts[0].astype(F32)
    for d in range(1, RING):
        value += parts[d].astype(F32)
    total[...] = value
    rounded[...] = value.astype(BF16)


def stack_sum(parts):
    shape = parts.shape[1:]
    return pl.pallas_call(
        stack_kernel,
        in_specs=[VMEM],
        out_specs=[VMEM] * 2,
        out_shape=[jax.ShapeDtypeStruct(shape, F32), jax.ShapeDtypeStruct(shape, BF16)],
        cost_estimate=cost(3 * parts.size, 4 * parts.size),
        compiler_params=params(8),
    )(parts)


def ring_kernel(own, a, b, c, total, rounded):
    value = own[...] + a[...].astype(F32) + b[...].astype(F32) + c[...].astype(F32)
    total[...] = value
    rounded[...] = value.astype(BF16)


def ring_sum(parts):
    shape = parts[0].shape
    return pl.pallas_call(
        ring_kernel,
        in_specs=[VMEM] * RING,
        out_specs=[VMEM] * 2,
        out_shape=[jax.ShapeDtypeStruct(shape, F32), jax.ShapeDtypeStruct(shape, BF16)],
        cost_estimate=cost(3 * shape[0] * shape[1], 16 * shape[0] * shape[1]),
        compiler_params=params(8),
    )(*parts)


def scale_kernel(total, far, rows, cols, out):
    value = total[...] + far[...].astype(F32)
    out[...] = (value / (rows[...] * cols[...] + damping)).astype(BF16)


def scale(total, far, rows, cols):
    return pl.pallas_call(
        scale_kernel,
        in_specs=[VMEM] * 4,
        out_specs=VMEM,
        out_shape=jax.ShapeDtypeStruct(total.shape, BF16),
        cost_estimate=cost(8 * total.size, 8 * total.size),
        compiler_params=params(8),
    )(total, far, rows, cols)


def add_up(parts):
    total = parts[0].astype(F32)
    for i in range(1, parts.shape[0]):
        total += parts[i].astype(F32)
    return total


def tie(*values):
    return lax.optimization_barrier(values)


def per_device(query_ids, layer_index, gradient, out_basis, in_basis, out_eigen, in_eigen):
    loops, reds = lax.axis_size("loop"), lax.axis_size("red")
    chips = loops // 2
    queries = query_ids.shape[0]
    chunk = queries // CHUNKS
    piece = chunk // RING
    core = lax.axis_index("loop") % 2
    x = lax.axis_index("red") % RING
    place = jnp.stack([core, x]).astype(jnp.int32)
    swap = [(i, i ^ 1) for i in range(loops)]
    flip = [(i, (i + RING) % reds) for i in range(reds)]
    rings = [[h + i for i in range(RING)] for h in range(0, reds, RING)]
    shift = [[(i, i - i % RING + (i + d) % RING) for i in range(reds)] for d in range(RING)]
    same_core = [[2 * i + c for i in range(chips)] for c in range(2)]

    def exchange(value):
        value = value.reshape(chips, -1, value.shape[1])
        return lax.all_to_all(value, "loop", 0, 0, axis_index_groups=same_core)

    got = lax.ppermute(gradient, "loop", swap)
    sel = select(query_ids, out_basis, chips)
    sel_got = lax.ppermute(sel, "loop", swap)
    part = partial_rows(place, sel, sel_got, gradient, got)
    part = exchange(part)
    eigen_rows = jnp.take(jnp.take(out_eigen, layer_index, axis=0)[0], query_ids)
    eigen_rows = eigen_rows.reshape(chips, 2, CHUNKS, -1).transpose(2, 1, 0, 3).reshape(CHUNKS, chunk)
    eigen_cols = jnp.take(in_eigen, layer_index, axis=0)
    factors = [
        lax.dynamic_slice_in_dim(eigen_rows[n], x * piece, piece, 0)[:, None] for n in range(CHUNKS)
    ]
    rows_w, *factors = tie(add_up(part).astype(BF16), *factors)
    share = rows_w.shape[0] // CHUNKS

    def gather(rows):
        rows = jnp.broadcast_to(rows[None], (chips,) + rows.shape).reshape(chunk, -1)
        return exchange(rows).reshape(chunk, -1)

    def ring(parts):
        return [parts[0]] + [lax.ppermute(parts[d], "red", shift[d]) for d in range(1, RING)]

    def swapped(value):
        return lax.ppermute(value, "loop", swap)

    own_a = gather(rows_w[:share])
    rows_b, own_a = tie(rows_w[share:], own_a)
    own_b = gather(rows_b)
    ring_a = ring(rotate(place, own_a, swapped(own_a), in_basis))
    own_b, *ring_a = tie(own_b, *ring_a)
    other_b = swapped(own_b)
    total_a, rounded_a = ring_sum(ring_a)
    far_a = lax.ppermute(rounded_a, "red", flip)
    other_b, total_a = tie(other_b, total_a)
    [rot_b] = rotate(place, own_b, other_b, in_basis, stacked=True)
    rot_b, far_a = tie(rot_b.reshape(RING, piece, -1), far_a)
    rot_b = lax.all_to_all(rot_b, "red", 0, 0, axis_index_groups=rings)
    scaled_a = scale(total_a, far_a, factors[0], eigen_cols)
    rot_b, *pieces_a = tie(rot_b, *ring([scaled_a] * RING))
    total_b, rounded_b = stack_sum(rot_b)
    far_b = lax.ppermute(rounded_b, "red", flip)
    pieces_a[0], total_b = tie(pieces_a[0], total_b)
    send_a, keep_a = back(place, pieces_a, in_basis)
    send_a, far_b = tie(send_a, far_b)
    part_a = join(keep_a, swapped(send_a))
    scaled_b = scale(total_b, far_b, factors[1], eigen_cols)
    pieces_b = ring([scaled_b] * RING)
    part_a = exchange(part_a)
    part_a, *pieces_b = tie(part_a, *pieces_b)
    send_b, keep_b = back(place, pieces_b, in_basis)
    part_b = exchange(join(keep_b, swapped(send_b)))
    return jnp.concatenate([add_up(part_a).astype(BF16), add_up(part_b).astype(BF16)], 0)


def solution(mesh):
    return jax.shard_map(
        per_device,
        mesh=mesh,
        in_specs=(
            P(),
            P(),
            P("loop", "red"),
            P("loop", None),
            P("red", "loop"),
            P(),
            P(None, "loop"),
        ),
        out_specs=P("loop", "red"),
        check_vma=False,
    )
```

```python
import functools

import jax
import jax.numpy as jnp
from jax import lax
from jax.experimental import pallas as pl
from jax.experimental.pallas import tpu as pltpu
from jax.sharding import PartitionSpec as P

damping = 0.05
CHUNKS = 2
RING = 4
F32, BF16 = jnp.float32, jnp.bfloat16
VMEM = pl.BlockSpec(memory_space=pltpu.VMEM)
ANY = pl.BlockSpec(memory_space=pl.ANY)
SMEM = pl.BlockSpec(memory_space=pltpu.SMEM)
NN = (((1,), (0,)), ((), ()))
NT = (((1,), (1,)), ((), ()))


def cost(flops, nbytes):
    return pl.CostEstimate(flops=flops, bytes_accessed=nbytes, transcendentals=0)


def dot(a, b, dims=NN):
    return lax.dot_general(a, b, dims, preferred_element_type=F32)


def params(mib):
    return pltpu.CompilerParams(vmem_limit_bytes=mib << 20)


def fixed(shape, at=(0, 0)):
    return pl.BlockSpec(shape, lambda *_: at)


def select_kernel(ids, basis, out, acc, *, chips):
    step = pl.program_id(0)
    width, queries = basis.shape[1], ids.shape[1]
    want = (ids[...] - step * width).astype(jnp.int16)
    lanes = lax.broadcasted_iota(jnp.int16, (width, queries), 0)
    hot = jnp.where(lanes == want, jnp.ones((), BF16), jnp.zeros((), BF16))
    part = dot(basis[...], hot)

    @pl.when(step == 0)
    def _():
        acc[...] = part

    @pl.when(step > 0)
    def _():
        acc[...] += part

    @pl.when(step == pl.num_programs(0) - 1)
    def _():
        rows = acc[...].T.astype(BF16)
        run = queries // chips // CHUNKS // 2
        for chip in range(chips):
            for core in range(2):
                for n in range(CHUNKS):
                    to = ((n * 2 + core) * chips + chip) * run
                    at = ((chip * 2 + core) * CHUNKS + n) * run
                    out[to : to + run, :] = rows[at : at + run, :]


def select(ids, basis, chips, block=2048):
    rows, width = basis.shape
    queries = ids.shape[0]
    return pl.pallas_call(
        functools.partial(select_kernel, chips=chips),
        grid=(width // block,),
        in_specs=[fixed((1, queries)), pl.BlockSpec((rows, block), lambda i: (0, i))],
        out_specs=fixed((queries, rows)),
        out_shape=jax.ShapeDtypeStruct((queries, rows), BF16),
        scratch_shapes=[pltpu.VMEM((rows, queries), F32)],
        cost_estimate=cost(2 * queries * rows * width, rows * width * 2),
        compiler_params=params(56),
    )(ids[None, :], basis)


def rows_kernel(place, sel, sel2, grad, grad2, out, buf, buf2, sems, *, chunk_index):
    steps = sems.shape[1]
    rows = pl.ds(chunk_index * out.shape[0], out.shape[0])
    half = out.shape[1]
    block = half // steps
    copies = []
    for i in range(steps):
        at = pl.ds(pl.multiple_of(place[0] * half + i * block, block), block)
        to = pl.ds(i * block, block)
        copies.append(
            [
                pltpu.make_async_copy(grad.at[:, at], buf.at[:, to], sems.at[0, i]),
                pltpu.make_async_copy(grad2.at[:, at], buf2.at[:, to], sems.at[1, i]),
            ]
        )
    for first, second in copies:
        first.start()
        second.start()
    for i in range(steps):
        to = pl.ds(i * block, block)
        copies[i][0].wait()
        copies[i][1].wait()
        total = dot(sel[rows, :], buf[:, to]) + dot(sel2[rows, :], buf2[:, to])
        out[:, to] = total.astype(BF16)


def partial_rows(place, sel, sel2, grad, grad2, chunk_index, steps=2):
    queries, units = sel.shape[0] // CHUNKS, sel.shape[1]
    half = grad.shape[1] // 2
    return pl.pallas_call(
        functools.partial(rows_kernel, chunk_index=chunk_index),
        in_specs=[SMEM, VMEM, VMEM, ANY, ANY],
        out_specs=VMEM,
        out_shape=jax.ShapeDtypeStruct((queries, half), BF16),
        scratch_shapes=[
            pltpu.VMEM((units, half), BF16),
            pltpu.VMEM((units, half), BF16),
            pltpu.SemaphoreType.DMA((2, steps)),
        ],
        cost_estimate=cost(4 * queries * units * half, 6 * queries * half),
        compiler_params=params(56),
    )(place, sel, sel2, grad, grad2)


def fetch(basis, buf, sems, cuts):
    copies = []
    for i, (start, size) in enumerate(cuts):
        at = pl.ds(start, size)
        copies.append(pltpu.make_async_copy(basis.at[at, :], buf.at[at, :], sems.at[i]))
    for copy in copies:
        copy.start()
    return copies


def rotate_kernel(place, own, other, basis, *refs, cuts):
    outs, (lhs, buf, acc, sems) = refs[:-4], refs[-4:]
    copies = fetch(basis, buf, sems, cuts)
    core, x = place[0], place[1] if len(outs) > 1 else 0
    piece, half = own.shape[0] // RING, own.shape[1]
    for d in range(RING):
        rows = pl.ds(pl.multiple_of(lax.rem(x + d, RING) * piece, piece), piece)
        to = pl.ds(d * piece, piece)
        lhs[core, to, :] = own[rows, :]
        lhs[1 - core, to, :] = other[rows, :]
    for i, (start, size) in enumerate(cuts):
        copies[i].wait()
        part = lhs[start // half, :, start % half : start % half + size]
        value = dot(part, buf[start : start + size, :])
        if i > 0:
            value += acc[...]
        if i < len(cuts) - 1:
            acc[...] = value
        elif len(outs) == 1:
            outs[0][...] = value.astype(BF16)
        else:
            for d in range(RING):
                outs[d][...] = value[d * piece : (d + 1) * piece].astype(outs[d].dtype)


def rotate(place, own, other, basis, stacked=False):
    m, half = other.shape
    k, n = basis.shape
    piece = m // RING
    outs = [jax.ShapeDtypeStruct((piece, n), F32 if d == 0 else BF16) for d in range(RING)]
    if stacked:
        outs = [jax.ShapeDtypeStruct((m, n), BF16)]
    block = half // 7
    cuts = [(h * half + at * block, size * block) for h in range(2) for at, size in ((0, 3), (3, 2), (5, 2))]
    return pl.pallas_call(
        functools.partial(rotate_kernel, cuts=cuts),
        in_specs=[SMEM, VMEM, VMEM, ANY],
        out_specs=[VMEM] * len(outs),
        out_shape=outs,
        scratch_shapes=[
            pltpu.VMEM((2, m, half), BF16),
            pltpu.VMEM((k, n), BF16),
            pltpu.VMEM((m, n), F32),
            pltpu.SemaphoreType.DMA((len(cuts),)),
        ],
        cost_estimate=cost(2 * m * k * n, 2 * k * n),
        compiler_params=params(50),
    )(place, own, other, basis)


def back_kernel(place, *refs, cuts):
    pieces, (basis, other, own, lhs, buf, send, keep, sems, out_sems) = refs[:RING], refs[RING:]
    copies = fetch(basis, buf, sems, cuts)
    core, x = place[0], place[1]
    piece = pieces[0].shape[0]
    for d in range(RING):
        to = lax.rem(x + RING - d + 2 * (1 - core), RING)
        lhs[pl.ds(pl.multiple_of(to * piece, piece), piece), :] = pieces[d][...]
    stores = []
    for i, (start, size) in enumerate(cuts):
        at = pl.ds(start, size)
        copies[i].wait()
        total = dot(lhs[...], buf[at, :], NT)
        send[:, at] = total[: 2 * piece].astype(BF16)
        keep[:, at] = total[2 * piece :]
        stores.append(pltpu.make_async_copy(send.at[:, at], other.at[:, at], out_sems.at[0, i]))
        stores[-1].start()
        stores.append(pltpu.make_async_copy(keep.at[:, at], own.at[:, at], out_sems.at[1, i]))
        stores[-1].start()
    for store in stores:
        store.wait()


def back(place, pieces, basis):
    piece, k = pieces[0].shape
    n = basis.shape[0]
    m = RING * piece
    cuts = [(i * n // 7, n // 7) for i in range(7)]
    return pl.pallas_call(
        functools.partial(back_kernel, cuts=cuts),
        in_specs=[SMEM] + [VMEM] * RING + [ANY],
        out_specs=[ANY] * 2,
        out_shape=[
            jax.ShapeDtypeStruct((m // 2, n), BF16),
            jax.ShapeDtypeStruct((m // 2, n), F32),
        ],
        scratch_shapes=[
            pltpu.VMEM((m, k), BF16),
            pltpu.VMEM((n, k), BF16),
            pltpu.VMEM((m // 2, n), BF16),
            pltpu.VMEM((m // 2, n), F32),
            pltpu.SemaphoreType.DMA((len(cuts),)),
            pltpu.SemaphoreType.DMA((2, len(cuts))),
        ],
        cost_estimate=cost(2 * m * k * n, 2 * k * n),
        compiler_params=params(50),
    )(place, *pieces, basis)


def join_kernel(keep, got, out):
    out[...] = (keep[...] + got[...].astype(F32)).astype(BF16)


def join(keep, got):
    return pl.pallas_call(
        join_kernel,
        in_specs=[VMEM] * 2,
        out_specs=VMEM,
        out_shape=jax.ShapeDtypeStruct(got.shape, BF16),
        cost_estimate=cost(2 * got.size, 8 * got.size),
        compiler_params=params(8),
    )(keep, got)


def stack_kernel(parts, total, rounded):
    value = parts[0].astype(F32)
    for d in range(1, RING):
        value += parts[d].astype(F32)
    total[...] = value
    rounded[...] = value.astype(BF16)


def stack_sum(parts):
    shape = parts.shape[1:]
    return pl.pallas_call(
        stack_kernel,
        in_specs=[VMEM],
        out_specs=[VMEM] * 2,
        out_shape=[jax.ShapeDtypeStruct(shape, F32), jax.ShapeDtypeStruct(shape, BF16)],
        cost_estimate=cost(3 * parts.size, 4 * parts.size),
        compiler_params=params(8),
    )(parts)


def ring_kernel(own, a, b, c, total, rounded):
    value = own[...] + a[...].astype(F32) + b[...].astype(F32) + c[...].astype(F32)
    total[...] = value
    rounded[...] = value.astype(BF16)


def ring_sum(parts):
    shape = parts[0].shape
    return pl.pallas_call(
        ring_kernel,
        in_specs=[VMEM] * RING,
        out_specs=[VMEM] * 2,
        out_shape=[jax.ShapeDtypeStruct(shape, F32), jax.ShapeDtypeStruct(shape, BF16)],
        cost_estimate=cost(3 * shape[0] * shape[1], 16 * shape[0] * shape[1]),
        compiler_params=params(8),
    )(*parts)


def scale_kernel(total, far, rows, cols, out):
    value = total[...] + far[...].astype(F32)
    out[...] = (value / (rows[...] * cols[...] + damping)).astype(BF16)


def scale(total, far, rows, cols):
    return pl.pallas_call(
        scale_kernel,
        in_specs=[VMEM] * 4,
        out_specs=VMEM,
        out_shape=jax.ShapeDtypeStruct(total.shape, BF16),
        cost_estimate=cost(8 * total.size, 8 * total.size),
        compiler_params=params(8),
    )(total, far, rows, cols)


def add_up(parts):
    total = parts[0].astype(F32)
    for i in range(1, parts.shape[0]):
        total += parts[i].astype(F32)
    return total


def tie(*values):
    return lax.optimization_barrier(values)


def per_device(query_ids, layer_index, gradient, out_basis, in_basis, out_eigen, in_eigen):
    loops, reds = lax.axis_size("loop"), lax.axis_size("red")
    chips = loops // 2
    queries = query_ids.shape[0]
    chunk = queries // CHUNKS
    piece = chunk // RING
    core = lax.axis_index("loop") % 2
    x = lax.axis_index("red") % RING
    place = jnp.stack([core, x]).astype(jnp.int32)
    swap = [(i, i ^ 1) for i in range(loops)]
    flip = [(i, (i + RING) % reds) for i in range(reds)]
    rings = [[h + i for i in range(RING)] for h in range(0, reds, RING)]
    shift = [[(i, i - i % RING + (i + d) % RING) for i in range(reds)] for d in range(RING)]
    same_core = [[2 * i + c for i in range(chips)] for c in range(2)]

    def exchange(value):
        value = value.reshape(chips, -1, value.shape[1])
        return lax.all_to_all(value, "loop", 0, 0, axis_index_groups=same_core)

    got = lax.ppermute(gradient, "loop", swap)
    sel = select(query_ids, out_basis, chips)
    sel_got = lax.ppermute(sel, "loop", swap)
    eigen_rows = jnp.take(jnp.take(out_eigen, layer_index, axis=0)[0], query_ids)
    eigen_rows = eigen_rows.reshape(chips, 2, CHUNKS, -1).transpose(2, 1, 0, 3).reshape(CHUNKS, chunk)
    eigen_cols = jnp.take(in_eigen, layer_index, axis=0)
    factors = [
        lax.dynamic_slice_in_dim(eigen_rows[n], x * piece, piece, 0)[:, None] for n in range(CHUNKS)
    ]

    def scatter(n):
        return partial_rows(place, sel, sel_got, gradient, got, n)

    def gather(parts):
        rows = add_up(parts).astype(BF16)
        rows = jnp.broadcast_to(rows[None], (chips,) + rows.shape).reshape(chunk, -1)
        return exchange(rows).reshape(chunk, -1)

    def ring(parts):
        return [parts[0]] + [lax.ppermute(parts[d], "red", shift[d]) for d in range(1, RING)]

    def swapped(value):
        return lax.ppermute(value, "loop", swap)

    part_a = scatter(0)
    part_a, *factors = tie(exchange(part_a), *factors)
    own_a = gather(part_a)
    part_b, own_a = tie(scatter(1), own_a)
    part_b = exchange(part_b)
    ring_a = ring(rotate(place, own_a, swapped(own_a), in_basis))
    part_b, *ring_a = tie(part_b, *ring_a)
    own_b = gather(part_b)
    total_a, rounded_a = ring_sum(ring_a)
    scaled_a = scale(total_a, lax.ppermute(rounded_a, "red", flip), factors[0], eigen_cols)
    own_b, scaled_a = tie(own_b, scaled_a)
    pieces_a = ring([scaled_a] * RING)
    ring_b = ring(rotate(place, own_b, swapped(own_b), in_basis))
    send_a, keep_a = back(place, pieces_a, in_basis)
    send_a, *ring_b = tie(send_a, *ring_b)
    total_b, rounded_b = ring_sum(ring_b)
    far_b = lax.ppermute(rounded_b, "red", flip)
    keep_a, far_b = tie(keep_a, far_b)
    part_a = join(keep_a, swapped(send_a))
    scaled_b = scale(total_b, far_b, factors[1], eigen_cols)
    part_a, *pieces_b = tie(exchange(part_a), *ring([scaled_b] * RING))
    send_b, keep_b = back(place, pieces_b, in_basis)
    part_b = exchange(join(keep_b, swapped(send_b)))
    return jnp.concatenate([add_up(part_a).astype(BF16), add_up(part_b).astype(BF16)], 0)


def solution(mesh):
    return jax.shard_map(
        per_device,
        mesh=mesh,
        in_specs=(
            P(),
            P(),
            P("loop", "red"),
            P("loop", None),
            P("red", "loop"),
            P(),
            P(None, "loop"),
        ),
        out_specs=P("loop", "red"),
        check_vma=False,
    )
```

```python
import functools

import jax
import jax.numpy as jnp
from jax import lax
from jax.experimental import pallas as pl
from jax.experimental.pallas import tpu as pltpu
from jax.sharding import PartitionSpec as P

damping = 0.05
CHUNKS = 2
RING = 4
F32, BF16 = jnp.float32, jnp.bfloat16
VMEM = pl.BlockSpec(memory_space=pltpu.VMEM)
ANY = pl.BlockSpec(memory_space=pl.ANY)
SMEM = pl.BlockSpec(memory_space=pltpu.SMEM)
NN = (((1,), (0,)), ((), ()))
NT = (((1,), (1,)), ((), ()))


def cost(flops, nbytes):
    return pl.CostEstimate(flops=flops, bytes_accessed=nbytes, transcendentals=0)


def dot(a, b, dims=NN):
    return lax.dot_general(a, b, dims, preferred_element_type=F32)


def params(mib):
    return pltpu.CompilerParams(vmem_limit_bytes=mib << 20)


def fixed(shape, at=(0, 0)):
    return pl.BlockSpec(shape, lambda *_: at)


def select_kernel(ids, basis, out, acc, *, chips):
    step = pl.program_id(0)
    width, queries = basis.shape[1], ids.shape[1]
    want = (ids[...] - step * width).astype(jnp.int16)
    lanes = lax.broadcasted_iota(jnp.int16, (width, queries), 0)
    hot = jnp.where(lanes == want, jnp.ones((), BF16), jnp.zeros((), BF16))
    part = dot(basis[...], hot)

    @pl.when(step == 0)
    def _():
        acc[...] = part

    @pl.when(step > 0)
    def _():
        acc[...] += part

    @pl.when(step == pl.num_programs(0) - 1)
    def _():
        rows = acc[...].T.astype(BF16)
        run = queries // chips // 2
        for chip in range(chips):
            for core in range(2):
                at, to = (chip * 2 + core) * run, (core * chips + chip) * run
                out[to : to + run, :] = rows[at : at + run, :]


def select(ids, basis, chips, block=2048):
    rows, width = basis.shape
    queries = ids.shape[1]
    return pl.pallas_call(
        functools.partial(select_kernel, chips=chips),
        grid=(width // block,),
        in_specs=[fixed((1, queries)), pl.BlockSpec((rows, block), lambda i: (0, i))],
        out_specs=fixed((queries, rows)),
        out_shape=jax.ShapeDtypeStruct((queries, rows), BF16),
        scratch_shapes=[pltpu.VMEM((rows, queries), F32)],
        cost_estimate=cost(2 * queries * rows * width, rows * width * 2),
        compiler_params=params(56),
    )(ids, basis)


def rows_kernel(place, sel, sel2, grad, grad2, out, buf, buf2, sems):
    steps = sems.shape[1]
    half = out.shape[1]
    block = half // steps
    copies = []
    for i in range(steps):
        at = pl.ds(pl.multiple_of(place[0] * half + i * block, block), block)
        to = pl.ds(i * block, block)
        copies.append(
            [
                pltpu.make_async_copy(grad.at[:, at], buf.at[:, to], sems.at[0, i]),
                pltpu.make_async_copy(grad2.at[:, at], buf2.at[:, to], sems.at[1, i]),
            ]
        )
    for first, second in copies:
        first.start()
        second.start()
    for i in range(steps):
        to = pl.ds(i * block, block)
        copies[i][0].wait()
        copies[i][1].wait()
        total = dot(sel[...], buf[:, to]) + dot(sel2[...], buf2[:, to])
        out[:, to] = total.astype(BF16)


def partial_rows(place, sel, sel2, grad, grad2, steps=2):
    queries, units = sel.shape
    half = grad.shape[1] // 2
    return pl.pallas_call(
        rows_kernel,
        in_specs=[SMEM, VMEM, VMEM, ANY, ANY],
        out_specs=VMEM,
        out_shape=jax.ShapeDtypeStruct((queries, half), BF16),
        scratch_shapes=[
            pltpu.VMEM((units, half), BF16),
            pltpu.VMEM((units, half), BF16),
            pltpu.SemaphoreType.DMA((2, steps)),
        ],
        cost_estimate=cost(4 * queries * units * half, 6 * queries * half),
        compiler_params=params(56),
    )(place, sel, sel2, grad, grad2)


def fetch(basis, buf, sems, cuts):
    copies = []
    for i, (start, size) in enumerate(cuts):
        at = pl.ds(start, size)
        copies.append(pltpu.make_async_copy(basis.at[at, :], buf.at[at, :], sems.at[i]))
    for copy in copies:
        copy.start()
    return copies


def rotate_kernel(place, own, other, basis, *refs, cuts):
    outs, (lhs, buf, acc, sems) = refs[:-4], refs[-4:]
    copies = fetch(basis, buf, sems, cuts)
    core, x = place[0], place[1] if len(outs) > 1 else 0
    piece, half = own.shape[0] // RING, own.shape[1]
    for d in range(RING):
        rows = pl.ds(pl.multiple_of(lax.rem(x + d, RING) * piece, piece), piece)
        to = pl.ds(d * piece, piece)
        lhs[core, to, :] = own[rows, :]
        lhs[1 - core, to, :] = other[rows, :]
    for i, (start, size) in enumerate(cuts):
        copies[i].wait()
        part = lhs[start // half, :, start % half : start % half + size]
        value = dot(part, buf[start : start + size, :])
        if i > 0:
            value += acc[...]
        if i < len(cuts) - 1:
            acc[...] = value
        elif len(outs) == 1:
            outs[0][...] = value.astype(BF16)
        else:
            for d in range(RING):
                outs[d][...] = value[d * piece : (d + 1) * piece].astype(outs[d].dtype)


def rotate(place, own, other, basis, stacked=False):
    m, half = other.shape
    k, n = basis.shape
    piece = m // RING
    outs = [jax.ShapeDtypeStruct((piece, n), F32 if d == 0 else BF16) for d in range(RING)]
    if stacked:
        outs = [jax.ShapeDtypeStruct((m, n), BF16)]
    block = half // 7
    cuts = [(h * half + at * block, size * block) for h in range(2) for at, size in ((0, 3), (3, 2), (5, 2))]
    return pl.pallas_call(
        functools.partial(rotate_kernel, cuts=cuts),
        in_specs=[SMEM, VMEM, VMEM, ANY],
        out_specs=[VMEM] * len(outs),
        out_shape=outs,
        scratch_shapes=[
            pltpu.VMEM((2, m, half), BF16),
            pltpu.VMEM((k, n), BF16),
            pltpu.VMEM((m, n), F32),
            pltpu.SemaphoreType.DMA((len(cuts),)),
        ],
        cost_estimate=cost(2 * m * k * n, 2 * k * n),
        compiler_params=params(50),
    )(place, own, other, basis)


def back_kernel(place, *refs, cuts):
    pieces, (basis, other, own, lhs, buf, send, keep, sems, out_sems) = refs[:RING], refs[RING:]
    copies = fetch(basis, buf, sems, cuts)
    core, x = place[0], place[1]
    piece = pieces[0].shape[0]
    for d in range(RING):
        to = lax.rem(x + RING - d + 2 * (1 - core), RING)
        lhs[pl.ds(pl.multiple_of(to * piece, piece), piece), :] = pieces[d][...]
    stores = []
    for i, (start, size) in enumerate(cuts):
        at = pl.ds(start, size)
        copies[i].wait()
        total = dot(lhs[...], buf[at, :], NT)
        send[:, at] = total[: 2 * piece].astype(BF16)
        keep[:, at] = total[2 * piece :]
        stores.append(pltpu.make_async_copy(send.at[:, at], other.at[:, at], out_sems.at[0, i]))
        stores[-1].start()
        stores.append(pltpu.make_async_copy(keep.at[:, at], own.at[:, at], out_sems.at[1, i]))
        stores[-1].start()
    for store in stores:
        store.wait()


def back(place, pieces, basis):
    piece, k = pieces[0].shape
    n = basis.shape[0]
    m = RING * piece
    cuts = [(i * n // 7, n // 7) for i in range(7)]
    return pl.pallas_call(
        functools.partial(back_kernel, cuts=cuts),
        in_specs=[SMEM] + [VMEM] * RING + [ANY],
        out_specs=[ANY] * 2,
        out_shape=[
            jax.ShapeDtypeStruct((m // 2, n), BF16),
            jax.ShapeDtypeStruct((m // 2, n), F32),
        ],
        scratch_shapes=[
            pltpu.VMEM((m, k), BF16),
            pltpu.VMEM((n, k), BF16),
            pltpu.VMEM((m // 2, n), BF16),
            pltpu.VMEM((m // 2, n), F32),
            pltpu.SemaphoreType.DMA((len(cuts),)),
            pltpu.SemaphoreType.DMA((2, len(cuts))),
        ],
        cost_estimate=cost(2 * m * k * n, 2 * k * n),
        compiler_params=params(50),
    )(place, *pieces, basis)


def join_kernel(keep, got, out):
    out[...] = (keep[...] + got[...].astype(F32)).astype(BF16)


def join(keep, got):
    return pl.pallas_call(
        join_kernel,
        in_specs=[VMEM] * 2,
        out_specs=VMEM,
        out_shape=jax.ShapeDtypeStruct(got.shape, BF16),
        cost_estimate=cost(2 * got.size, 8 * got.size),
        compiler_params=params(8),
    )(keep, got)


def spread_kernel(parts, out):
    value = parts[0].astype(F32)
    for i in range(1, parts.shape[0]):
        value += parts[i].astype(F32)
    value = value.astype(BF16)
    for i in range(parts.shape[0]):
        out[i] = value


def spread(parts):
    return pl.pallas_call(
        spread_kernel,
        in_specs=[VMEM],
        out_specs=VMEM,
        out_shape=jax.ShapeDtypeStruct(parts.shape, BF16),
        cost_estimate=cost(parts.size, 4 * parts.size),
        compiler_params=params(12),
    )(parts)


def ring_kernel(own, a, b, c, total, rounded):
    value = own[...] + a[...].astype(F32) + b[...].astype(F32) + c[...].astype(F32)
    total[...] = value
    rounded[...] = value.astype(BF16)


def ring_sum(parts):
    shape = parts[0].shape
    return pl.pallas_call(
        ring_kernel,
        in_specs=[VMEM] * RING,
        out_specs=[VMEM] * 2,
        out_shape=[jax.ShapeDtypeStruct(shape, F32), jax.ShapeDtypeStruct(shape, BF16)],
        cost_estimate=cost(3 * shape[0] * shape[1], 16 * shape[0] * shape[1]),
        compiler_params=params(8),
    )(*parts)


def scale_kernel(total, far, rows, cols, out):
    value = total[...] + far[...].astype(F32)
    out[...] = (value / (rows[...] * cols[...] + damping)).astype(BF16)


def scale(total, far, rows, cols):
    return pl.pallas_call(
        scale_kernel,
        in_specs=[VMEM] * 4,
        out_specs=VMEM,
        out_shape=jax.ShapeDtypeStruct(total.shape, BF16),
        cost_estimate=cost(8 * total.size, 8 * total.size),
        compiler_params=params(8),
    )(total, far, rows, cols)


def add_up(parts):
    total = parts[0].astype(F32)
    for i in range(1, parts.shape[0]):
        total += parts[i].astype(F32)
    return total


def tie(*values):
    return lax.optimization_barrier(values)


def per_device(query_ids, layer_index, gradient, out_basis, in_basis, out_eigen, in_eigen):
    loops, reds = lax.axis_size("loop"), lax.axis_size("red")
    chips = loops // 2
    queries = query_ids.shape[0]
    chunk = queries // CHUNKS
    piece = chunk // RING
    core = lax.axis_index("loop") % 2
    x = lax.axis_index("red") % RING
    place = jnp.stack([core, x]).astype(jnp.int32)
    swap = [(i, i ^ 1) for i in range(loops)]
    flip = [(i, (i + RING) % reds) for i in range(reds)]
    shift = [[(i, i - i % RING + (i + d) % RING) for i in range(reds)] for d in range(RING)]
    same_core = [[2 * i + c for i in range(chips)] for c in range(2)]

    def exchange(value):
        value = value.reshape(chips, -1, value.shape[1])
        return lax.all_to_all(value, "loop", 0, 0, axis_index_groups=same_core)

    got = lax.ppermute(gradient, "loop", swap)
    ids = query_ids.reshape(loops, CHUNKS, -1).transpose(1, 0, 2).reshape(CHUNKS, 1, chunk)
    eigen_rows = jnp.take(jnp.take(out_eigen, layer_index, axis=0)[0], query_ids)
    eigen_rows = eigen_rows.reshape(chips, 2, CHUNKS, -1).transpose(2, 1, 0, 3).reshape(CHUNKS, chunk)
    eigen_cols = jnp.take(in_eigen, layer_index, axis=0)
    factors = [
        lax.dynamic_slice_in_dim(eigen_rows[n], x * piece, piece, 0)[:, None] for n in range(CHUNKS)
    ]

    def scatter(ids):
        sel = select(ids, out_basis, chips)
        return partial_rows(place, sel, lax.ppermute(sel, "loop", swap), gradient, got)

    def gather(parts):
        return exchange(spread(parts).reshape(chunk, -1)).reshape(chunk, -1)

    def ring(parts):
        got = {d: lax.ppermute(parts[d], "red", shift[d]) for d in (2, 1, 3)}
        return [parts[0]] + [got[d] for d in range(1, RING)]

    def swapped(value):
        return lax.ppermute(value, "loop", swap)

    part_a = scatter(ids[0])
    part_a, ids_b, *factors = tie(exchange(part_a), ids[1], *factors)
    own_a = gather(part_a)
    part_b, own_a = tie(scatter(ids_b), own_a)
    part_b = exchange(part_b)
    ring_a = ring(rotate(place, own_a, swapped(own_a), in_basis))
    part_b, *ring_a = tie(part_b, *ring_a)
    own_b = gather(part_b)
    total_a, rounded_a = ring_sum(ring_a)
    scaled_a = scale(total_a, lax.ppermute(rounded_a, "red", flip), factors[0], eigen_cols)
    own_b, scaled_a = tie(own_b, scaled_a)
    pieces_a = ring([scaled_a] * RING)
    ring_b = ring(rotate(place, own_b, swapped(own_b), in_basis))
    send_a, keep_a = back(place, pieces_a, in_basis)
    send_a, *ring_b = tie(send_a, *ring_b)
    total_b, rounded_b = ring_sum(ring_b)
    far_b = lax.ppermute(rounded_b, "red", flip)
    keep_a, far_b = tie(keep_a, far_b)
    part_a = join(keep_a, swapped(send_a))
    scaled_b = scale(total_b, far_b, factors[1], eigen_cols)
    part_a, *pieces_b = tie(exchange(part_a), *ring([scaled_b] * RING))
    send_b, keep_b = back(place, pieces_b, in_basis)
    part_b = exchange(join(keep_b, swapped(send_b)))
    return jnp.concatenate([add_up(part_a).astype(BF16), add_up(part_b).astype(BF16)], 0)


def solution(mesh):
    return jax.shard_map(
        per_device,
        mesh=mesh,
        in_specs=(
            P(),
            P(),
            P("loop", "red"),
            P("loop", None),
            P("red", "loop"),
            P(),
            P(None, "loop"),
        ),
        out_specs=P("loop", "red"),
        check_vma=False,
    )
```

```python
import functools

import jax
import jax.numpy as jnp
from jax import lax
from jax.experimental import pallas as pl
from jax.experimental.pallas import tpu as pltpu
from jax.sharding import PartitionSpec as P

damping = 0.05
CHUNKS = 2
RING = 4
F32, BF16 = jnp.float32, jnp.bfloat16
VMEM = pl.BlockSpec(memory_space=pltpu.VMEM)
ANY = pl.BlockSpec(memory_space=pl.ANY)
SMEM = pl.BlockSpec(memory_space=pltpu.SMEM)
NN = (((1,), (0,)), ((), ()))
NT = (((1,), (1,)), ((), ()))


def cost(flops, nbytes):
    return pl.CostEstimate(flops=flops, bytes_accessed=nbytes, transcendentals=0)


def dot(a, b, dims=NN):
    return lax.dot_general(a, b, dims, preferred_element_type=F32)


def params(mib):
    return pltpu.CompilerParams(vmem_limit_bytes=mib << 20)


def fixed(shape, at=(0, 0)):
    return pl.BlockSpec(shape, lambda *_: at)


def select_kernel(ids, basis, out, acc, *, chips):
    step = pl.program_id(0)
    width, queries = basis.shape[1], ids.shape[1]
    want = (ids[...] - step * width).astype(jnp.int16)
    lanes = lax.broadcasted_iota(jnp.int16, (width, queries), 0)
    hot = jnp.where(lanes == want, jnp.ones((), BF16), jnp.zeros((), BF16))
    part = dot(basis[...], hot)

    @pl.when(step == 0)
    def _():
        acc[...] = part

    @pl.when(step > 0)
    def _():
        acc[...] += part

    @pl.when(step == pl.num_programs(0) - 1)
    def _():
        rows = acc[...].T.astype(BF16)
        share = queries // chips // CHUNKS
        run = share // 2
        for chip in range(chips):
            for core in range(2):
                for n in range(CHUNKS):
                    at = (core * chips + chip) * run
                    to = at // share * (share * CHUNKS) + n * share + at % share
                    at = ((chip * 2 + core) * CHUNKS + n) * run
                    out[to : to + run, :] = rows[at : at + run, :]


def select(ids, basis, chips, block=2048):
    rows, width = basis.shape
    queries = ids.shape[0]
    return pl.pallas_call(
        functools.partial(select_kernel, chips=chips),
        grid=(width // block,),
        in_specs=[fixed((1, queries)), pl.BlockSpec((rows, block), lambda i: (0, i))],
        out_specs=fixed((queries, rows)),
        out_shape=jax.ShapeDtypeStruct((queries, rows), BF16),
        scratch_shapes=[pltpu.VMEM((rows, queries), F32)],
        cost_estimate=cost(2 * queries * rows * width, rows * width * 2),
        compiler_params=params(56),
    )(ids[None, :], basis)


def rows_kernel(place, sel, sel2, grad, grad2, out, buf, buf2, sems):
    steps = sems.shape[1]
    half = out.shape[1]
    block = half // steps
    copies = []
    for i in range(steps):
        at = pl.ds(pl.multiple_of(place[0] * half + i * block, block), block)
        to = pl.ds(i * block, block)
        copies.append(
            [
                pltpu.make_async_copy(grad.at[:, at], buf.at[:, to], sems.at[0, i]),
                pltpu.make_async_copy(grad2.at[:, at], buf2.at[:, to], sems.at[1, i]),
            ]
        )
    for first, second in copies:
        first.start()
        second.start()
    for i in range(steps):
        to = pl.ds(i * block, block)
        copies[i][0].wait()
        copies[i][1].wait()
        total = dot(sel[...], buf[:, to]) + dot(sel2[...], buf2[:, to])
        out[:, to] = total.astype(BF16)


def partial_rows(place, sel, sel2, grad, grad2, steps=2):
    queries, units = sel.shape
    half = grad.shape[1] // 2
    return pl.pallas_call(
        rows_kernel,
        in_specs=[SMEM, VMEM, VMEM, ANY, ANY],
        out_specs=VMEM,
        out_shape=jax.ShapeDtypeStruct((queries, half), BF16),
        scratch_shapes=[
            pltpu.VMEM((units, half), BF16),
            pltpu.VMEM((units, half), BF16),
            pltpu.SemaphoreType.DMA((2, steps)),
        ],
        cost_estimate=cost(4 * queries * units * half, 6 * queries * half),
        compiler_params=params(56),
    )(place, sel, sel2, grad, grad2)


def fetch(basis, buf, sems, cuts):
    copies = []
    for i, (start, size) in enumerate(cuts):
        at = pl.ds(start, size)
        copies.append(pltpu.make_async_copy(basis.at[at, :], buf.at[at, :], sems.at[i]))
    for copy in copies:
        copy.start()
    return copies


def rotate_kernel(place, own, other, basis, *refs, cuts):
    outs, (lhs, buf, acc, sems) = refs[:-4], refs[-4:]
    copies = fetch(basis, buf, sems, cuts)
    core, x = place[0], place[1] if len(outs) > 1 else 0
    piece, half = own.shape[0] // RING, own.shape[1]
    for d in range(RING):
        rows = pl.ds(pl.multiple_of(lax.rem(x + d, RING) * piece, piece), piece)
        to = pl.ds(d * piece, piece)
        lhs[core, to, :] = own[rows, :]
        lhs[1 - core, to, :] = other[rows, :]
    for i, (start, size) in enumerate(cuts):
        copies[i].wait()
        part = lhs[start // half, :, start % half : start % half + size]
        value = dot(part, buf[start : start + size, :])
        if i > 0:
            value += acc[...]
        if i < len(cuts) - 1:
            acc[...] = value
        elif len(outs) == 1:
            outs[0][...] = value.astype(BF16)
        else:
            for d in range(RING):
                outs[d][...] = value[d * piece : (d + 1) * piece].astype(outs[d].dtype)


def rotate(place, own, other, basis, stacked=False):
    m, half = other.shape
    k, n = basis.shape
    piece = m // RING
    outs = [jax.ShapeDtypeStruct((piece, n), F32 if d == 0 else BF16) for d in range(RING)]
    if stacked:
        outs = [jax.ShapeDtypeStruct((m, n), BF16)]
    block = half // 7
    cuts = [(h * half + at * block, size * block) for h in range(2) for at, size in ((0, 3), (3, 2), (5, 2))]
    return pl.pallas_call(
        functools.partial(rotate_kernel, cuts=cuts),
        in_specs=[SMEM, VMEM, VMEM, ANY],
        out_specs=[VMEM] * len(outs),
        out_shape=outs,
        scratch_shapes=[
            pltpu.VMEM((2, m, half), BF16),
            pltpu.VMEM((k, n), BF16),
            pltpu.VMEM((m, n), F32),
            pltpu.SemaphoreType.DMA((len(cuts),)),
        ],
        cost_estimate=cost(2 * m * k * n, 2 * k * n),
        compiler_params=params(50),
    )(place, own, other, basis)


def back_kernel(place, *refs, cuts):
    pieces, (basis, other, own, lhs, buf, send, keep, sems, out_sems) = refs[:RING], refs[RING:]
    copies = fetch(basis, buf, sems, cuts)
    core, x = place[0], place[1]
    piece = pieces[0].shape[0]
    for d in range(RING):
        to = lax.rem(x + RING - d + 2 * (1 - core), RING)
        lhs[pl.ds(pl.multiple_of(to * piece, piece), piece), :] = pieces[d][...]
    stores = []
    for i, (start, size) in enumerate(cuts):
        at = pl.ds(start, size)
        copies[i].wait()
        total = dot(lhs[...], buf[at, :], NT)
        send[:, at] = total[: 2 * piece].astype(BF16)
        keep[:, at] = total[2 * piece :]
        stores.append(pltpu.make_async_copy(send.at[:, at], other.at[:, at], out_sems.at[0, i]))
        stores[-1].start()
        stores.append(pltpu.make_async_copy(keep.at[:, at], own.at[:, at], out_sems.at[1, i]))
        stores[-1].start()
    for store in stores:
        store.wait()


def back(place, pieces, basis):
    piece, k = pieces[0].shape
    n = basis.shape[0]
    m = RING * piece
    cuts = [(i * n // 7, n // 7) for i in range(7)]
    return pl.pallas_call(
        functools.partial(back_kernel, cuts=cuts),
        in_specs=[SMEM] + [VMEM] * RING + [ANY],
        out_specs=[ANY] * 2,
        out_shape=[
            jax.ShapeDtypeStruct((m // 2, n), BF16),
            jax.ShapeDtypeStruct((m // 2, n), F32),
        ],
        scratch_shapes=[
            pltpu.VMEM((m, k), BF16),
            pltpu.VMEM((n, k), BF16),
            pltpu.VMEM((m // 2, n), BF16),
            pltpu.VMEM((m // 2, n), F32),
            pltpu.SemaphoreType.DMA((len(cuts),)),
            pltpu.SemaphoreType.DMA((2, len(cuts))),
        ],
        cost_estimate=cost(2 * m * k * n, 2 * k * n),
        compiler_params=params(50),
    )(place, *pieces, basis)


def join_kernel(*refs):
    out = refs[-1]
    run = out.shape[1] // CHUNKS
    for n in range(CHUNKS):
        total = (refs[2 * n][...] + refs[2 * n + 1][...].astype(F32)).astype(BF16)
        for chip in range(out.shape[0]):
            out[chip, n * run : (n + 1) * run, :] = total[chip * run : (chip + 1) * run]


def join(parts, chips):
    rows, width = parts[0].shape
    return pl.pallas_call(
        join_kernel,
        in_specs=[VMEM] * len(parts),
        out_specs=VMEM,
        out_shape=jax.ShapeDtypeStruct((chips, CHUNKS * rows // chips, width), BF16),
        cost_estimate=cost(4 * rows * width, 16 * rows * width),
        compiler_params=params(24),
    )(*parts)


def stack_kernel(parts, total, rounded):
    value = parts[0].astype(F32)
    for d in range(1, RING):
        value += parts[d].astype(F32)
    total[...] = value
    rounded[...] = value.astype(BF16)


def stack_sum(parts):
    shape = parts.shape[1:]
    return pl.pallas_call(
        stack_kernel,
        in_specs=[VMEM],
        out_specs=[VMEM] * 2,
        out_shape=[jax.ShapeDtypeStruct(shape, F32), jax.ShapeDtypeStruct(shape, BF16)],
        cost_estimate=cost(3 * parts.size, 4 * parts.size),
        compiler_params=params(8),
    )(parts)


def ring_kernel(own, a, b, c, total, rounded):
    value = own[...] + a[...].astype(F32) + b[...].astype(F32) + c[...].astype(F32)
    total[...] = value
    rounded[...] = value.astype(BF16)


def ring_sum(parts):
    shape = parts[0].shape
    return pl.pallas_call(
        ring_kernel,
        in_specs=[VMEM] * RING,
        out_specs=[VMEM] * 2,
        out_shape=[jax.ShapeDtypeStruct(shape, F32), jax.ShapeDtypeStruct(shape, BF16)],
        cost_estimate=cost(3 * shape[0] * shape[1], 16 * shape[0] * shape[1]),
        compiler_params=params(8),
    )(*parts)


def scale_kernel(total, far, rows, cols, out):
    value = total[...] + far[...].astype(F32)
    out[...] = (value / (rows[...] * cols[...] + damping)).astype(BF16)


def scale(total, far, rows, cols):
    return pl.pallas_call(
        scale_kernel,
        in_specs=[VMEM] * 4,
        out_specs=VMEM,
        out_shape=jax.ShapeDtypeStruct(total.shape, BF16),
        cost_estimate=cost(8 * total.size, 8 * total.size),
        compiler_params=params(8),
    )(total, far, rows, cols)


def add_up(parts):
    total = parts[0].astype(F32)
    for i in range(1, parts.shape[0]):
        total += parts[i].astype(F32)
    return total


def tie(*values):
    return lax.optimization_barrier(values)


def per_device(query_ids, layer_index, gradient, out_basis, in_basis, out_eigen, in_eigen):
    loops, reds = lax.axis_size("loop"), lax.axis_size("red")
    chips = loops // 2
    queries = query_ids.shape[0]
    chunk = queries // CHUNKS
    piece = chunk // RING
    core = lax.axis_index("loop") % 2
    x = lax.axis_index("red") % RING
    place = jnp.stack([core, x]).astype(jnp.int32)
    swap = [(i, i ^ 1) for i in range(loops)]
    flip = [(i, (i + RING) % reds) for i in range(reds)]
    rings = [[h + i for i in range(RING)] for h in range(0, reds, RING)]
    shift = [[(i, i - i % RING + (i + d) % RING) for i in range(reds)] for d in range(RING)]
    same_core = [[2 * i + c for i in range(chips)] for c in range(2)]

    def exchange(value):
        value = value.reshape(chips, -1, value.shape[-1])
        return lax.all_to_all(value, "loop", 0, 0, axis_index_groups=same_core)

    got = lax.ppermute(gradient, "loop", swap)
    sel = select(query_ids, out_basis, chips)
    sel_got = lax.ppermute(sel, "loop", swap)
    part = partial_rows(place, sel, sel_got, gradient, got)
    part = exchange(part)
    eigen_rows = jnp.take(jnp.take(out_eigen, layer_index, axis=0)[0], query_ids)
    eigen_rows = eigen_rows.reshape(chips, 2, CHUNKS, -1).transpose(2, 1, 0, 3).reshape(CHUNKS, chunk)
    eigen_cols = jnp.take(in_eigen, layer_index, axis=0)
    factors = [
        lax.dynamic_slice_in_dim(eigen_rows[n], x * piece, piece, 0)[:, None] for n in range(CHUNKS)
    ]
    rows_w, *factors = tie(add_up(part).astype(BF16), *factors)
    share = rows_w.shape[0] // CHUNKS

    def gather(rows):
        rows = jnp.broadcast_to(rows[None], (chips,) + rows.shape).reshape(chunk, -1)
        return exchange(rows).reshape(chunk, -1)

    def ring(parts):
        return [parts[0]] + [lax.ppermute(parts[d], "red", shift[d]) for d in range(1, RING)]

    def swapped(value):
        return lax.ppermute(value, "loop", swap)

    own_a = gather(rows_w[:share])
    rows_b, own_a = tie(rows_w[share:], own_a)
    own_b = gather(rows_b)
    rot_a = list(rotate(place, own_a, swapped(own_a), in_basis))
    ring_a = ring(rot_a)
    own_b, ring_a[2] = tie(own_b, ring_a[2])
    ring_b = ring(rotate(place, own_b, swapped(own_b), in_basis))
    total_a, rounded_a = ring_sum(ring_a)
    total_a, *ring_b = tie(total_a, *ring_b)
    far_a = lax.ppermute(rounded_a, "red", flip)
    total_b, rounded_b = ring_sum(ring_b)
    far_a, total_b = tie(far_a, total_b)
    scaled_a = scale(total_a, far_a, factors[0], eigen_cols)
    pieces_a = ring([scaled_a] * RING)
    far_b = lax.ppermute(rounded_b, "red", flip)
    far_b, *pieces_a = tie(far_b, *pieces_a)
    scaled_b = scale(total_b, far_b, factors[1], eigen_cols)
    pieces_b = ring([scaled_b] * RING)
    send_a, keep_a = back(place, pieces_a, in_basis)
    pieces_b[0], send_a = tie(pieces_b[0], send_a)
    send_b, keep_b = back(place, pieces_b, in_basis)
    part = join([keep_a, swapped(send_a), keep_b, swapped(send_b)], chips)
    return add_up(exchange(part)).astype(BF16)


def solution(mesh):
    return jax.shard_map(
        per_device,
        mesh=mesh,
        in_specs=(
            P(),
            P(),
            P("loop", "red"),
            P("loop", None),
            P("red", "loop"),
            P(),
            P(None, "loop"),
        ),
        out_specs=P("loop", "red"),
        check_vma=False,
    )
```

```python
import functools

import jax
import jax.numpy as jnp
from jax import lax
from jax.experimental import pallas as pl
from jax.experimental.pallas import tpu as pltpu
from jax.sharding import PartitionSpec as P

damping = 0.05
CHUNKS = 2
RING = 4
F32, BF16 = jnp.float32, jnp.bfloat16
VMEM = pl.BlockSpec(memory_space=pltpu.VMEM)
ANY = pl.BlockSpec(memory_space=pl.ANY)
SMEM = pl.BlockSpec(memory_space=pltpu.SMEM)
NN = (((1,), (0,)), ((), ()))
NT = (((1,), (1,)), ((), ()))


def cost(flops, nbytes):
    return pl.CostEstimate(flops=flops, bytes_accessed=nbytes, transcendentals=0)


def dot(a, b, dims=NN):
    return lax.dot_general(a, b, dims, preferred_element_type=F32)


def params(mib):
    return pltpu.CompilerParams(vmem_limit_bytes=mib << 20)


def fixed(shape, at=(0, 0)):
    return pl.BlockSpec(shape, lambda *_: at)


def select_kernel(ids, basis, out, acc, *, chips):
    step = pl.program_id(0)
    width, queries = basis.shape[1], ids.shape[1]
    want = (ids[...] - step * width).astype(jnp.int16)
    lanes = lax.broadcasted_iota(jnp.int16, (width, queries), 0)
    hot = jnp.where(lanes == want, jnp.ones((), BF16), jnp.zeros((), BF16))
    part = dot(basis[...], hot)

    @pl.when(step == 0)
    def _():
        acc[...] = part

    @pl.when(step > 0)
    def _():
        acc[...] += part

    @pl.when(step == pl.num_programs(0) - 1)
    def _():
        rows = acc[...].T.astype(BF16)
        share = queries // chips // CHUNKS
        run = share // 2
        for chip in range(chips):
            for core in range(2):
                for n in range(CHUNKS):
                    at = (core * chips + chip) * run
                    to = at // share * (share * CHUNKS) + n * share + at % share
                    at = ((chip * 2 + core) * CHUNKS + n) * run
                    out[to : to + run, :] = rows[at : at + run, :]


def select(ids, basis, chips, block=2048):
    rows, width = basis.shape
    queries = ids.shape[0]
    return pl.pallas_call(
        functools.partial(select_kernel, chips=chips),
        grid=(width // block,),
        in_specs=[fixed((1, queries)), pl.BlockSpec((rows, block), lambda i: (0, i))],
        out_specs=fixed((queries, rows)),
        out_shape=jax.ShapeDtypeStruct((queries, rows), BF16),
        scratch_shapes=[pltpu.VMEM((rows, queries), F32)],
        cost_estimate=cost(2 * queries * rows * width, rows * width * 2),
        compiler_params=params(56),
    )(ids[None, :], basis)


def rows_kernel(place, sel, sel2, grad, grad2, out, buf, buf2, sems):
    steps = sems.shape[1]
    half = out.shape[1]
    block = half // steps
    copies = []
    for i in range(steps):
        at = pl.ds(pl.multiple_of(place[0] * half + i * block, block), block)
        to = pl.ds(i * block, block)
        copies.append(
            [
                pltpu.make_async_copy(grad.at[:, at], buf.at[:, to], sems.at[0, i]),
                pltpu.make_async_copy(grad2.at[:, at], buf2.at[:, to], sems.at[1, i]),
            ]
        )
    for first, second in copies:
        first.start()
        second.start()
    for i in range(steps):
        to = pl.ds(i * block, block)
        copies[i][0].wait()
        copies[i][1].wait()
        total = dot(sel[...], buf[:, to]) + dot(sel2[...], buf2[:, to])
        out[:, to] = total.astype(BF16)


def partial_rows(place, sel, sel2, grad, grad2, steps=7):
    queries, units = sel.shape
    half = grad.shape[1] // 2
    return pl.pallas_call(
        rows_kernel,
        in_specs=[SMEM, VMEM, VMEM, ANY, ANY],
        out_specs=VMEM,
        out_shape=jax.ShapeDtypeStruct((queries, half), BF16),
        scratch_shapes=[
            pltpu.VMEM((units, half), BF16),
            pltpu.VMEM((units, half), BF16),
            pltpu.SemaphoreType.DMA((2, steps)),
        ],
        cost_estimate=cost(4 * queries * units * half, 6 * queries * half),
        compiler_params=params(56),
    )(place, sel, sel2, grad, grad2)


def fetch(basis, buf, sems, cuts):
    copies = []
    for i, (start, size) in enumerate(cuts):
        at = pl.ds(start, size)
        copies.append(pltpu.make_async_copy(basis.at[at, :], buf.at[at, :], sems.at[i]))
    for copy in copies:
        copy.start()
    return copies


def rotate_kernel(place, own, other, basis, *refs, cuts):
    outs, (lhs, buf, acc, sems) = refs[:-4], refs[-4:]
    copies = fetch(basis, buf, sems, cuts)
    core, x = place[0], place[1] if len(outs) > 1 else 0
    piece, half = own.shape[0] // RING, own.shape[1]
    for d in range(RING):
        rows = pl.ds(pl.multiple_of(lax.rem(x + d, RING) * piece, piece), piece)
        to = pl.ds(d * piece, piece)
        lhs[core, to, :] = own[rows, :]
        lhs[1 - core, to, :] = other[rows, :]
    for i, (start, size) in enumerate(cuts):
        copies[i].wait()
        part = lhs[start // half, :, start % half : start % half + size]
        value = dot(part, buf[start : start + size, :])
        if i > 0:
            value += acc[...]
        if i < len(cuts) - 1:
            acc[...] = value
        elif len(outs) == 1:
            outs[0][...] = value.astype(BF16)
        else:
            for d in range(RING):
                outs[d][...] = value[d * piece : (d + 1) * piece].astype(outs[d].dtype)


def rotate(place, own, other, basis, stacked=False):
    m, half = other.shape
    k, n = basis.shape
    piece = m // RING
    outs = [jax.ShapeDtypeStruct((piece, n), F32 if d == 0 else BF16) for d in range(RING)]
    if stacked:
        outs = [jax.ShapeDtypeStruct((m, n), BF16)]
    block = half // 7
    cuts = [(h * half + at * block, size * block) for h in range(2) for at, size in ((0, 3), (3, 2), (5, 2))]
    return pl.pallas_call(
        functools.partial(rotate_kernel, cuts=cuts),
        in_specs=[SMEM, VMEM, VMEM, ANY],
        out_specs=[VMEM] * len(outs),
        out_shape=outs,
        scratch_shapes=[
            pltpu.VMEM((2, m, half), BF16),
            pltpu.VMEM((k, n), BF16),
            pltpu.VMEM((m, n), F32),
            pltpu.SemaphoreType.DMA((len(cuts),)),
        ],
        cost_estimate=cost(2 * m * k * n, 2 * k * n),
        compiler_params=params(50),
    )(place, own, other, basis)


def back_kernel(place, *refs, cuts):
    pieces, (basis, other, own, lhs, buf, send, keep, sems, out_sems) = refs[:RING], refs[RING:]
    copies = fetch(basis, buf, sems, cuts)
    core, x = place[0], place[1]
    piece = pieces[0].shape[0]
    for d in range(RING):
        to = lax.rem(x + RING - d + 2 * (1 - core), RING)
        lhs[pl.ds(pl.multiple_of(to * piece, piece), piece), :] = pieces[d][...]
    stores = []
    for i, (start, size) in enumerate(cuts):
        at = pl.ds(start, size)
        copies[i].wait()
        total = dot(lhs[...], buf[at, :], NT)
        send[:, at] = total[: 2 * piece].astype(BF16)
        keep[:, at] = total[2 * piece :]
        stores.append(pltpu.make_async_copy(send.at[:, at], other.at[:, at], out_sems.at[0, i]))
        stores[-1].start()
        stores.append(pltpu.make_async_copy(keep.at[:, at], own.at[:, at], out_sems.at[1, i]))
        stores[-1].start()
    for store in stores:
        store.wait()


def back(place, pieces, basis):
    piece, k = pieces[0].shape
    n = basis.shape[0]
    m = RING * piece
    cuts = [(i * n // 7, n // 7) for i in range(7)]
    return pl.pallas_call(
        functools.partial(back_kernel, cuts=cuts),
        in_specs=[SMEM] + [VMEM] * RING + [ANY],
        out_specs=[ANY] * 2,
        out_shape=[
            jax.ShapeDtypeStruct((m // 2, n), BF16),
            jax.ShapeDtypeStruct((m // 2, n), F32),
        ],
        scratch_shapes=[
            pltpu.VMEM((m, k), BF16),
            pltpu.VMEM((n, k), BF16),
            pltpu.VMEM((m // 2, n), BF16),
            pltpu.VMEM((m // 2, n), F32),
            pltpu.SemaphoreType.DMA((len(cuts),)),
            pltpu.SemaphoreType.DMA((2, len(cuts))),
        ],
        cost_estimate=cost(2 * m * k * n, 2 * k * n),
        compiler_params=params(50),
    )(place, *pieces, basis)


def join_kernel(*refs):
    out = refs[-1]
    run = out.shape[1] // CHUNKS
    for n in range(CHUNKS):
        total = (refs[2 * n][...] + refs[2 * n + 1][...].astype(F32)).astype(BF16)
        for chip in range(out.shape[0]):
            out[chip, n * run : (n + 1) * run, :] = total[chip * run : (chip + 1) * run]


def join(parts, chips):
    rows, width = parts[0].shape
    return pl.pallas_call(
        join_kernel,
        in_specs=[VMEM] * len(parts),
        out_specs=VMEM,
        out_shape=jax.ShapeDtypeStruct((chips, CHUNKS * rows // chips, width), BF16),
        cost_estimate=cost(4 * rows * width, 16 * rows * width),
        compiler_params=params(24),
    )(*parts)


def stack_kernel(parts, total, rounded):
    value = parts[0].astype(F32)
    for d in range(1, RING):
        value += parts[d].astype(F32)
    total[...] = value
    rounded[...] = value.astype(BF16)


def stack_sum(parts):
    shape = parts.shape[1:]
    return pl.pallas_call(
        stack_kernel,
        in_specs=[VMEM],
        out_specs=[VMEM] * 2,
        out_shape=[jax.ShapeDtypeStruct(shape, F32), jax.ShapeDtypeStruct(shape, BF16)],
        cost_estimate=cost(3 * parts.size, 4 * parts.size),
        compiler_params=params(8),
    )(parts)


def ring_kernel(own, a, b, c, total, rounded):
    value = own[...] + a[...].astype(F32) + b[...].astype(F32) + c[...].astype(F32)
    total[...] = value
    rounded[...] = value.astype(BF16)


def ring_sum(parts):
    shape = parts[0].shape
    return pl.pallas_call(
        ring_kernel,
        in_specs=[VMEM] * RING,
        out_specs=[VMEM] * 2,
        out_shape=[jax.ShapeDtypeStruct(shape, F32), jax.ShapeDtypeStruct(shape, BF16)],
        cost_estimate=cost(3 * shape[0] * shape[1], 16 * shape[0] * shape[1]),
        compiler_params=params(8),
    )(*parts)


def scale_kernel(total, far, rows, cols, out):
    value = total[...] + far[...].astype(F32)
    out[...] = (value / (rows[...] * cols[...] + damping)).astype(BF16)


def scale(total, far, rows, cols):
    return pl.pallas_call(
        scale_kernel,
        in_specs=[VMEM] * 4,
        out_specs=VMEM,
        out_shape=jax.ShapeDtypeStruct(total.shape, BF16),
        cost_estimate=cost(8 * total.size, 8 * total.size),
        compiler_params=params(8),
    )(total, far, rows, cols)


def add_up(parts):
    total = parts[0].astype(F32)
    for i in range(1, parts.shape[0]):
        total += parts[i].astype(F32)
    return total


def tie(*values):
    return lax.optimization_barrier(values)


def per_device(query_ids, layer_index, gradient, out_basis, in_basis, out_eigen, in_eigen):
    loops, reds = lax.axis_size("loop"), lax.axis_size("red")
    chips = loops // 2
    queries = query_ids.shape[0]
    chunk = queries // CHUNKS
    piece = chunk // RING
    half = gradient.shape[1] // 2
    core = lax.axis_index("loop") % 2
    x = lax.axis_index("red") % RING
    place = jnp.stack([core, x]).astype(jnp.int32)
    swap = [(i, i ^ 1) for i in range(loops)]
    flip = [(i, (i + RING) % reds) for i in range(reds)]
    rings = [[h + i for i in range(RING)] for h in range(0, reds, RING)]
    shift = [[(i, i - i % RING + (i + d) % RING) for i in range(reds)] for d in range(RING)]
    same_core = [[2 * i + c for i in range(chips)] for c in range(2)]

    def exchange(value):
        value = value.reshape(chips, -1, value.shape[-1])
        return lax.all_to_all(value, "loop", 0, 0, axis_index_groups=same_core)

    got = lax.ppermute(gradient, "loop", swap)
    sel = select(query_ids, out_basis, chips)
    sel_got = lax.ppermute(sel, "loop", swap)
    part = partial_rows(place, sel, sel_got, gradient, got)
    part = exchange(part)
    eigen_rows = jnp.take(jnp.take(out_eigen, layer_index, axis=0)[0], query_ids)
    eigen_rows = eigen_rows.reshape(chips, 2, CHUNKS, -1).transpose(2, 1, 0, 3).reshape(CHUNKS, chunk)
    eigen_cols = jnp.take(in_eigen, layer_index, axis=0)
    factors = [
        lax.dynamic_slice_in_dim(eigen_rows[n], x * piece, piece, 0)[:, None] for n in range(CHUNKS)
    ]
    rows_w, *factors = tie(add_up(part).astype(BF16), *factors)
    share = rows_w.shape[0] // CHUNKS

    def copied(rows):
        return jnp.broadcast_to(rows[None], (chips,) + rows.shape).reshape(chunk, half)

    def ring(parts):
        return [parts[0]] + [lax.ppermute(parts[d], "red", shift[d]) for d in range(1, RING)]

    def swapped(value):
        return lax.ppermute(value, "loop", swap)

    own_a = exchange(copied(rows_w[:share])).reshape(chunk, half)
    rows_b, own_a = tie(copied(rows_w[share:]), own_a)
    own_b = exchange(rows_b).reshape(chunk, half)
    rot_a = list(rotate(place, own_a, swapped(own_a), in_basis))
    own_b, rot_a[0] = tie(own_b, rot_a[0])
    ring_a = ring(rot_a)
    ring_b = ring(rotate(place, own_b, swapped(own_b), in_basis))
    total_a, rounded_a = ring_sum(ring_a)
    total_a, *ring_b = tie(total_a, *ring_b)
    far_a = lax.ppermute(rounded_a, "red", flip)
    total_b, rounded_b = ring_sum(ring_b)
    far_a, total_b = tie(far_a, total_b)
    scaled_a = scale(total_a, far_a, factors[0], eigen_cols)
    pieces_a = ring([scaled_a] * RING)
    far_b = lax.ppermute(rounded_b, "red", flip)
    scaled_b = scale(total_b, far_b, factors[1], eigen_cols)
    pieces_b = ring([scaled_b] * RING)
    send_a, keep_a = back(place, pieces_a, in_basis)
    pieces_b[0], send_a = tie(pieces_b[0], send_a)
    send_b, keep_b = back(place, pieces_b, in_basis)
    part = join([keep_a, swapped(send_a), keep_b, swapped(send_b)], chips)
    return add_up(exchange(part)).astype(BF16)


def solution(mesh):
    return jax.shard_map(
        per_device,
        mesh=mesh,
        in_specs=(
            P(),
            P(),
            P("loop", "red"),
            P("loop", None),
            P("red", "loop"),
            P(),
            P(None, "loop"),
        ),
        out_specs=P("loop", "red"),
        check_vma=False,
    )
```

```python
import functools

import jax
import jax.numpy as jnp
from jax import lax
from jax.experimental import pallas as pl
from jax.experimental.pallas import tpu as pltpu
from jax.sharding import PartitionSpec as P

damping = 0.05
CHUNKS = 2
RING = 4
F32, BF16 = jnp.float32, jnp.bfloat16
VMEM = pl.BlockSpec(memory_space=pltpu.VMEM)
ANY = pl.BlockSpec(memory_space=pl.ANY)
SMEM = pl.BlockSpec(memory_space=pltpu.SMEM)
NN = (((1,), (0,)), ((), ()))
NT = (((1,), (1,)), ((), ()))


def cost(flops, nbytes):
    return pl.CostEstimate(flops=flops, bytes_accessed=nbytes, transcendentals=0)


def dot(a, b, dims=NN):
    return lax.dot_general(a, b, dims, preferred_element_type=F32)


def params(mib):
    return pltpu.CompilerParams(vmem_limit_bytes=mib << 20)


def fixed(shape, at=(0, 0)):
    return pl.BlockSpec(shape, lambda *_: at)


def select_kernel(ids, basis, out, acc, *, chips):
    step = pl.program_id(0)
    width, queries = basis.shape[1], ids.shape[1]
    want = (ids[...] - step * width).astype(jnp.int16)
    lanes = lax.broadcasted_iota(jnp.int16, (width, queries), 0)
    hot = jnp.where(lanes == want, jnp.ones((), BF16), jnp.zeros((), BF16))
    part = dot(basis[...], hot)

    @pl.when(step == 0)
    def _():
        acc[...] = part

    @pl.when(step > 0)
    def _():
        acc[...] += part

    @pl.when(step == pl.num_programs(0) - 1)
    def _():
        rows = acc[...].T.astype(BF16)
        share = queries // chips // CHUNKS
        run = share // 2
        for chip in range(chips):
            for core in range(2):
                for n in range(CHUNKS):
                    at = (core * chips + chip) * run
                    to = at // share * (share * CHUNKS) + n * share + at % share
                    at = ((chip * 2 + core) * CHUNKS + n) * run
                    out[to : to + run, :] = rows[at : at + run, :]


def select(ids, basis, chips, block=4096):
    rows, width = basis.shape
    queries = ids.shape[0]
    return pl.pallas_call(
        functools.partial(select_kernel, chips=chips),
        grid=(width // block,),
        in_specs=[fixed((1, queries)), pl.BlockSpec((rows, block), lambda i: (0, i))],
        out_specs=fixed((queries, rows)),
        out_shape=jax.ShapeDtypeStruct((queries, rows), BF16),
        scratch_shapes=[pltpu.VMEM((rows, queries), F32)],
        cost_estimate=cost(2 * queries * rows * width, rows * width * 2),
        compiler_params=params(56),
    )(ids[None, :], basis)


def rows_kernel(place, sel, sel2, grad, grad2, out, buf, buf2, sems):
    steps = sems.shape[1]
    half = out.shape[1]
    block = half // steps
    copies = []
    for i in range(steps):
        at = pl.ds(pl.multiple_of(place[0] * half + i * block, block), block)
        to = pl.ds(i * block, block)
        copies.append(
            [
                pltpu.make_async_copy(grad.at[:, at], buf.at[:, to], sems.at[0, i]),
                pltpu.make_async_copy(grad2.at[:, at], buf2.at[:, to], sems.at[1, i]),
            ]
        )
    for first, second in copies:
        first.start()
        second.start()
    for i in range(steps):
        to = pl.ds(i * block, block)
        copies[i][0].wait()
        copies[i][1].wait()
        total = dot(sel[...], buf[:, to]) + dot(sel2[...], buf2[:, to])
        out[:, to] = total.astype(BF16)


def partial_rows(place, sel, sel2, grad, grad2, steps=2):
    queries, units = sel.shape
    half = grad.shape[1] // 2
    return pl.pallas_call(
        rows_kernel,
        in_specs=[SMEM, VMEM, VMEM, ANY, ANY],
        out_specs=VMEM,
        out_shape=jax.ShapeDtypeStruct((queries, half), BF16),
        scratch_shapes=[
            pltpu.VMEM((units, half), BF16),
            pltpu.VMEM((units, half), BF16),
            pltpu.SemaphoreType.DMA((2, steps)),
        ],
        cost_estimate=cost(4 * queries * units * half, 6 * queries * half),
        compiler_params=params(56),
    )(place, sel, sel2, grad, grad2)


def fetch(basis, buf, sems, cuts):
    copies = []
    for i, (start, size) in enumerate(cuts):
        at = pl.ds(start, size)
        copies.append(pltpu.make_async_copy(basis.at[at, :], buf.at[at, :], sems.at[i]))
    for copy in copies:
        copy.start()
    return copies


def rotate_kernel(place, own, other, basis, *refs, cuts):
    outs, (lhs, buf, acc, sems) = refs[:-4], refs[-4:]
    copies = fetch(basis, buf, sems, cuts)
    core, x = place[0], place[1]
    piece, half = own.shape[0] // RING, own.shape[1]
    for d in range(RING):
        rows = pl.ds(pl.multiple_of(lax.rem(x + d, RING) * piece, piece), piece)
        to = pl.ds(d * piece, piece)
        lhs[core, to, :] = own[rows, :]
        lhs[1 - core, to, :] = other[rows, :]
    for i, (start, size) in enumerate(cuts):
        copies[i].wait()
        part = lhs[start // half, :, start % half : start % half + size]
        value = dot(part, buf[start : start + size, :])
        if i > 0:
            value += acc[...]
        if i < len(cuts) - 1:
            acc[...] = value
        else:
            for d in range(RING):
                outs[d][...] = value[d * piece : (d + 1) * piece].astype(outs[d].dtype)


def rotate(place, own, other, basis):
    m, half = other.shape
    k, n = basis.shape
    piece = m // RING
    outs = [jax.ShapeDtypeStruct((piece, n), F32 if d == 0 else BF16) for d in range(RING)]
    block = half // 7
    cuts = [(h * half + at * block, size * block) for h in range(2) for at, size in ((0, 3), (3, 2), (5, 2))]
    return pl.pallas_call(
        functools.partial(rotate_kernel, cuts=cuts),
        in_specs=[SMEM, VMEM, VMEM, ANY],
        out_specs=[VMEM] * len(outs),
        out_shape=outs,
        scratch_shapes=[
            pltpu.VMEM((2, m, half), BF16),
            pltpu.VMEM((k, n), BF16),
            pltpu.VMEM((m, n), F32),
            pltpu.SemaphoreType.DMA((len(cuts),)),
        ],
        cost_estimate=cost(2 * m * k * n, 2 * k * n),
        compiler_params=params(50),
    )(place, own, other, basis)


def back_kernel(place, *refs, cuts):
    pieces, (basis, other, own, lhs, buf, send, keep, sems, out_sems) = refs[:RING], refs[RING:]
    copies = fetch(basis, buf, sems, cuts)
    core, x = place[0], place[1]
    piece = pieces[0].shape[0]
    for d in range(RING):
        to = lax.rem(x + RING - d + 2 * (1 - core), RING)
        lhs[pl.ds(pl.multiple_of(to * piece, piece), piece), :] = pieces[d][...]
    stores = []
    for i, (start, size) in enumerate(cuts):
        at = pl.ds(start, size)
        copies[i].wait()
        total = dot(lhs[...], buf[at, :], NT)
        send[:, at] = total[: 2 * piece].astype(BF16)
        keep[:, at] = total[2 * piece :]
        stores.append(pltpu.make_async_copy(send.at[:, at], other.at[:, at], out_sems.at[0, i]))
        stores[-1].start()
        stores.append(pltpu.make_async_copy(keep.at[:, at], own.at[:, at], out_sems.at[1, i]))
        stores[-1].start()
    for store in stores:
        store.wait()


def back(place, pieces, basis):
    piece, k = pieces[0].shape
    n = basis.shape[0]
    m = RING * piece
    cuts = [(i * n // 7, n // 7) for i in range(7)]
    return pl.pallas_call(
        functools.partial(back_kernel, cuts=cuts),
        in_specs=[SMEM] + [VMEM] * RING + [ANY],
        out_specs=[ANY] * 2,
        out_shape=[
            jax.ShapeDtypeStruct((m // 2, n), BF16),
            jax.ShapeDtypeStruct((m // 2, n), F32),
        ],
        scratch_shapes=[
            pltpu.VMEM((m, k), BF16),
            pltpu.VMEM((n, k), BF16),
            pltpu.VMEM((m // 2, n), BF16),
            pltpu.VMEM((m // 2, n), F32),
            pltpu.SemaphoreType.DMA((len(cuts),)),
            pltpu.SemaphoreType.DMA((2, len(cuts))),
        ],
        cost_estimate=cost(2 * m * k * n, 2 * k * n),
        compiler_params=params(50),
    )(place, *pieces, basis)


def join_kernel(*refs):
    out = refs[-1]
    run = out.shape[1] // CHUNKS
    for n in range(CHUNKS):
        total = (refs[2 * n][...] + refs[2 * n + 1][...].astype(F32)).astype(BF16)
        for chip in range(out.shape[0]):
            out[chip, n * run : (n + 1) * run, :] = total[chip * run : (chip + 1) * run]


def join(parts, chips):
    rows, width = parts[0].shape
    return pl.pallas_call(
        join_kernel,
        in_specs=[VMEM] * len(parts),
        out_specs=VMEM,
        out_shape=jax.ShapeDtypeStruct((chips, CHUNKS * rows // chips, width), BF16),
        cost_estimate=cost(4 * rows * width, 16 * rows * width),
        compiler_params=params(24),
    )(*parts)


def ring_kernel(own, a, b, c, total, rounded):
    value = own[...] + a[...].astype(F32) + b[...].astype(F32) + c[...].astype(F32)
    total[...] = value
    rounded[...] = value.astype(BF16)


def ring_sum(parts):
    shape = parts[0].shape
    return pl.pallas_call(
        ring_kernel,
        in_specs=[VMEM] * RING,
        out_specs=[VMEM] * 2,
        out_shape=[jax.ShapeDtypeStruct(shape, F32), jax.ShapeDtypeStruct(shape, BF16)],
        cost_estimate=cost(3 * shape[0] * shape[1], 16 * shape[0] * shape[1]),
        compiler_params=params(8),
    )(*parts)


def scale_kernel(total, far, rows, cols, out):
    value = total[...] + far[...].astype(F32)
    out[...] = (value / (rows[...] * cols[...] + damping)).astype(BF16)


def scale(total, far, rows, cols):
    return pl.pallas_call(
        scale_kernel,
        in_specs=[VMEM] * 4,
        out_specs=VMEM,
        out_shape=jax.ShapeDtypeStruct(total.shape, BF16),
        cost_estimate=cost(8 * total.size, 8 * total.size),
        compiler_params=params(8),
    )(total, far, rows, cols)


def add_up(parts):
    total = parts[0].astype(F32)
    for i in range(1, parts.shape[0]):
        total += parts[i].astype(F32)
    return total


def tie(*values):
    return lax.optimization_barrier(values)


def per_device(query_ids, layer_index, gradient, out_basis, in_basis, out_eigen, in_eigen):
    loops, reds = lax.axis_size("loop"), lax.axis_size("red")
    chips = loops // 2
    queries = query_ids.shape[0]
    chunk = queries // CHUNKS
    piece = chunk // RING
    half = gradient.shape[1] // 2
    core = lax.axis_index("loop") % 2
    x = lax.axis_index("red") % RING
    place = jnp.stack([core, x]).astype(jnp.int32)
    swap = [(i, i ^ 1) for i in range(loops)]
    flip = [(i, (i + RING) % reds) for i in range(reds)]
    shift = [[(i, i - i % RING + (i + d) % RING) for i in range(reds)] for d in range(RING)]
    same_core = [[2 * i + c for i in range(chips)] for c in range(2)]

    def exchange(value):
        value = value.reshape(chips, -1, value.shape[-1])
        return lax.all_to_all(value, "loop", 0, 0, axis_index_groups=same_core)

    got = lax.ppermute(gradient, "loop", swap)
    sel = select(query_ids, out_basis, chips)
    sel_got = lax.ppermute(sel, "loop", swap)
    part = partial_rows(place, sel, sel_got, gradient, got)
    part = exchange(part)
    eigen_rows = jnp.take(jnp.take(out_eigen, layer_index, axis=0)[0], query_ids)
    eigen_rows = eigen_rows.reshape(chips, 2, CHUNKS, -1).transpose(2, 1, 0, 3).reshape(CHUNKS, chunk)
    eigen_cols = jnp.take(in_eigen, layer_index, axis=0)
    factors = [
        lax.dynamic_slice_in_dim(eigen_rows[n], x * piece, piece, 0)[:, None] for n in range(CHUNKS)
    ]
    rows_w, *factors = tie(add_up(part).astype(BF16), *factors)
    share = rows_w.shape[0] // CHUNKS

    def copied(rows):
        return jnp.broadcast_to(rows[None], (chips,) + rows.shape).reshape(chunk, half)

    def ring(parts):
        return [parts[0]] + [lax.ppermute(parts[d], "red", shift[d]) for d in range(1, RING)]

    def swapped(value):
        return lax.ppermute(value, "loop", swap)

    own_a = exchange(copied(rows_w[:share])).reshape(chunk, half)
    rows_b, own_a = tie(copied(rows_w[share:]), own_a)
    own_b = exchange(rows_b).reshape(chunk, half)
    rot_a = list(rotate(place, own_a, swapped(own_a), in_basis))
    own_b, rot_a[0] = tie(own_b, rot_a[0])
    ring_a = ring(rot_a)
    ring_b = ring(rotate(place, own_b, swapped(own_b), in_basis))
    total_a, rounded_a = ring_sum(ring_a)
    total_a, *ring_b = tie(total_a, *ring_b)
    far_a = lax.ppermute(rounded_a, "red", flip)
    total_b, rounded_b = ring_sum(ring_b)
    far_a, total_b = tie(far_a, total_b)
    scaled_a = scale(total_a, far_a, factors[0], eigen_cols)
    pieces_a = ring([scaled_a] * RING)
    far_b = lax.ppermute(rounded_b, "red", flip)
    scaled_b = scale(total_b, far_b, factors[1], eigen_cols)
    pieces_b = ring([scaled_b] * RING)
    send_a, keep_a = back(place, pieces_a, in_basis)
    pieces_b[0], send_a = tie(pieces_b[0], send_a)
    send_b, keep_b = back(place, pieces_b, in_basis)
    part = join([keep_a, swapped(send_a), keep_b, swapped(send_b)], chips)
    return add_up(exchange(part)).astype(BF16)


def solution(mesh):
    return jax.shard_map(
        per_device,
        mesh=mesh,
        in_specs=(
            P(),
            P(),
            P("loop", "red"),
            P("loop", None),
            P("red", "loop"),
            P(),
            P(None, "loop"),
        ),
        out_specs=P("loop", "red"),
        check_vma=False,
    )
```

```python
import functools

import jax
import jax.numpy as jnp
from jax import lax
from jax.experimental import pallas as pl
from jax.experimental.pallas import tpu as pltpu
from jax.sharding import PartitionSpec as P

damping = 0.05
CHUNKS = 2
RING = 4
F32, BF16 = jnp.float32, jnp.bfloat16
VMEM = pl.BlockSpec(memory_space=pltpu.VMEM)
ANY = pl.BlockSpec(memory_space=pl.ANY)
SMEM = pl.BlockSpec(memory_space=pltpu.SMEM)
NN = (((1,), (0,)), ((), ()))
NT = (((1,), (1,)), ((), ()))


def cost(flops, nbytes):
    return pl.CostEstimate(flops=flops, bytes_accessed=nbytes, transcendentals=0)


def dot(a, b, dims=NN):
    return lax.dot_general(a, b, dims, preferred_element_type=F32)


def params(mib):
    return pltpu.CompilerParams(vmem_limit_bytes=mib << 20)


def fixed(shape, at=(0, 0)):
    return pl.BlockSpec(shape, lambda *_: at)


def select_kernel(ids, basis, out, acc, *, chips):
    step = pl.program_id(0)
    width, queries = basis.shape[1], ids.shape[1]
    want = (ids[...] - step * width).astype(jnp.int16)
    lanes = lax.broadcasted_iota(jnp.int16, (width, queries), 0)
    hot = jnp.where(lanes == want, jnp.ones((), BF16), jnp.zeros((), BF16))
    part = dot(basis[...], hot)

    @pl.when(step == 0)
    def _():
        acc[...] = part

    @pl.when(step > 0)
    def _():
        acc[...] += part

    @pl.when(step == pl.num_programs(0) - 1)
    def _():
        rows = acc[...].T.astype(BF16)
        share = queries // chips // CHUNKS
        run = share // 2
        for chip in range(chips):
            for core in range(2):
                for n in range(CHUNKS):
                    at = (core * chips + chip) * run
                    to = at // share * (share * CHUNKS) + n * share + at % share
                    at = ((chip * 2 + core) * CHUNKS + n) * run
                    out[to : to + run, :] = rows[at : at + run, :]


def select(ids, basis, chips, block=4096):
    rows, width = basis.shape
    queries = ids.shape[0]
    return pl.pallas_call(
        functools.partial(select_kernel, chips=chips),
        grid=(width // block,),
        in_specs=[fixed((1, queries)), pl.BlockSpec((rows, block), lambda i: (0, i))],
        out_specs=fixed((queries, rows)),
        out_shape=jax.ShapeDtypeStruct((queries, rows), BF16),
        scratch_shapes=[pltpu.VMEM((rows, queries), F32)],
        cost_estimate=cost(2 * queries * rows * width, rows * width * 2),
        compiler_params=params(56),
    )(ids[None, :], basis)


def rows_kernel(place, sel, sel2, grad, grad2, out, buf, buf2, sems):
    steps = sems.shape[1]
    half = out.shape[1]
    block = half // steps
    copies = []
    for i in range(steps):
        at = pl.ds(pl.multiple_of(place[0] * half + i * block, block), block)
        to = pl.ds(i * block, block)
        copies.append(
            [
                pltpu.make_async_copy(grad.at[:, at], buf.at[:, to], sems.at[0, i]),
                pltpu.make_async_copy(grad2.at[:, at], buf2.at[:, to], sems.at[1, i]),
            ]
        )
    for first, second in copies:
        first.start()
        second.start()
    for i in range(steps):
        to = pl.ds(i * block, block)
        copies[i][0].wait()
        copies[i][1].wait()
        total = dot(sel[...], buf[:, to]) + dot(sel2[...], buf2[:, to])
        out[:, to] = total.astype(BF16)


def partial_rows(place, sel, sel2, grad, grad2, steps=2):
    queries, units = sel.shape
    half = grad.shape[1] // 2
    return pl.pallas_call(
        rows_kernel,
        in_specs=[SMEM, VMEM, VMEM, ANY, ANY],
        out_specs=VMEM,
        out_shape=jax.ShapeDtypeStruct((queries, half), BF16),
        scratch_shapes=[
            pltpu.VMEM((units, half), BF16),
            pltpu.VMEM((units, half), BF16),
            pltpu.SemaphoreType.DMA((2, steps)),
        ],
        cost_estimate=cost(4 * queries * units * half, 6 * queries * half),
        compiler_params=params(50),
    )(place, sel, sel2, grad, grad2)


def fetch(basis, buf, sems, cuts):
    copies = []
    for i, (start, size) in enumerate(cuts):
        at = pl.ds(start, size)
        copies.append(pltpu.make_async_copy(basis.at[at, :], buf.at[at, :], sems.at[i]))
    for copy in copies:
        copy.start()
    return copies


def rotate_kernel(place, own, other, basis, *refs, cuts):
    outs, (lhs, buf, acc, sems) = refs[:-4], refs[-4:]
    copies = fetch(basis, buf, sems, cuts)
    core, x = place[0], place[1]
    piece, half = own.shape[0] // RING, own.shape[1]
    for d in range(RING):
        rows = pl.ds(pl.multiple_of(lax.rem(x + d, RING) * piece, piece), piece)
        to = pl.ds(d * piece, piece)
        lhs[core, to, :] = own[rows, :]
        lhs[1 - core, to, :] = other[rows, :]
    for i, (start, size) in enumerate(cuts):
        copies[i].wait()
        part = lhs[start // half, :, start % half : start % half + size]
        value = dot(part, buf[start : start + size, :])
        if i > 0:
            value += acc[...]
        if i < len(cuts) - 1:
            acc[...] = value
        else:
            for d in range(RING):
                outs[d][...] = value[d * piece : (d + 1) * piece].astype(outs[d].dtype)


def rotate(place, own, other, basis):
    m, half = other.shape
    k, n = basis.shape
    piece = m // RING
    outs = [jax.ShapeDtypeStruct((piece, n), F32 if d == 0 else BF16) for d in range(RING)]
    block = half // 7
    cuts = [(h * half + at * block, size * block) for h in range(2) for at, size in ((0, 3), (3, 2), (5, 2))]
    return pl.pallas_call(
        functools.partial(rotate_kernel, cuts=cuts),
        in_specs=[SMEM, VMEM, VMEM, ANY],
        out_specs=[VMEM] * len(outs),
        out_shape=outs,
        scratch_shapes=[
            pltpu.VMEM((2, m, half), BF16),
            pltpu.VMEM((k, n), BF16),
            pltpu.VMEM((m, n), F32),
            pltpu.SemaphoreType.DMA((len(cuts),)),
        ],
        cost_estimate=cost(2 * m * k * n, 2 * k * n),
        compiler_params=params(50),
    )(place, own, other, basis)


def back_kernel(place, *refs, cuts):
    pieces, (basis, other, own, lhs, buf, send, keep, sems, out_sems) = refs[:RING], refs[RING:]
    copies = fetch(basis, buf, sems, cuts)
    core, x = place[0], place[1]
    piece = pieces[0].shape[0]
    for d in range(RING):
        to = lax.rem(x + RING - d + 2 * (1 - core), RING)
        lhs[pl.ds(pl.multiple_of(to * piece, piece), piece), :] = pieces[d][...]
    stores = []
    for i, (start, size) in enumerate(cuts):
        at = pl.ds(start, size)
        copies[i].wait()
        total = dot(lhs[...], buf[at, :], NT)
        send[:, at] = total[: 2 * piece].astype(BF16)
        keep[:, at] = total[2 * piece :]
        stores.append(pltpu.make_async_copy(send.at[:, at], other.at[:, at], out_sems.at[0, i]))
        stores[-1].start()
        stores.append(pltpu.make_async_copy(keep.at[:, at], own.at[:, at], out_sems.at[1, i]))
        stores[-1].start()
    for store in stores:
        store.wait()


def back(place, pieces, basis):
    piece, k = pieces[0].shape
    n = basis.shape[0]
    m = RING * piece
    cuts = [(i * n // 7, n // 7) for i in range(7)]
    return pl.pallas_call(
        functools.partial(back_kernel, cuts=cuts),
        in_specs=[SMEM] + [VMEM] * RING + [ANY],
        out_specs=[ANY] * 2,
        out_shape=[
            jax.ShapeDtypeStruct((m // 2, n), BF16),
            jax.ShapeDtypeStruct((m // 2, n), F32),
        ],
        scratch_shapes=[
            pltpu.VMEM((m, k), BF16),
            pltpu.VMEM((n, k), BF16),
            pltpu.VMEM((m // 2, n), BF16),
            pltpu.VMEM((m // 2, n), F32),
            pltpu.SemaphoreType.DMA((len(cuts),)),
            pltpu.SemaphoreType.DMA((2, len(cuts))),
        ],
        cost_estimate=cost(2 * m * k * n, 2 * k * n),
        compiler_params=params(50),
    )(place, *pieces, basis)


def join_kernel(*refs):
    out = refs[-1]
    run = out.shape[1] // CHUNKS
    for n in range(CHUNKS):
        total = (refs[2 * n][...] + refs[2 * n + 1][...].astype(F32)).astype(BF16)
        for chip in range(out.shape[0]):
            out[chip, n * run : (n + 1) * run, :] = total[chip * run : (chip + 1) * run]


def join(parts, chips):
    rows, width = parts[0].shape
    return pl.pallas_call(
        join_kernel,
        in_specs=[VMEM] * len(parts),
        out_specs=VMEM,
        out_shape=jax.ShapeDtypeStruct((chips, CHUNKS * rows // chips, width), BF16),
        cost_estimate=cost(4 * rows * width, 16 * rows * width),
        compiler_params=params(24),
    )(*parts)


def ring_kernel(own, a, b, c, total, rounded):
    value = own[...] + a[...].astype(F32) + b[...].astype(F32) + c[...].astype(F32)
    total[...] = value
    rounded[...] = value.astype(BF16)


def ring_sum(parts):
    shape = parts[0].shape
    return pl.pallas_call(
        ring_kernel,
        in_specs=[VMEM] * RING,
        out_specs=[VMEM] * 2,
        out_shape=[jax.ShapeDtypeStruct(shape, F32), jax.ShapeDtypeStruct(shape, BF16)],
        cost_estimate=cost(3 * shape[0] * shape[1], 16 * shape[0] * shape[1]),
        compiler_params=params(8),
    )(*parts)


def scale_kernel(total, far, rows, cols, out):
    value = total[...] + far[...].astype(F32)
    out[...] = (value / (rows[...] * cols[...] + damping)).astype(BF16)


def scale(total, far, rows, cols):
    return pl.pallas_call(
        scale_kernel,
        in_specs=[VMEM] * 4,
        out_specs=VMEM,
        out_shape=jax.ShapeDtypeStruct(total.shape, BF16),
        cost_estimate=cost(8 * total.size, 8 * total.size),
        compiler_params=params(8),
    )(total, far, rows, cols)


def add_up(parts):
    total = parts[0].astype(F32)
    for i in range(1, parts.shape[0]):
        total += parts[i].astype(F32)
    return total


def tie(*values):
    return lax.optimization_barrier(values)


def per_device(query_ids, layer_index, gradient, out_basis, in_basis, out_eigen, in_eigen):
    loops, reds = lax.axis_size("loop"), lax.axis_size("red")
    chips = loops // 2
    queries = query_ids.shape[0]
    chunk = queries // CHUNKS
    piece = chunk // RING
    half = gradient.shape[1] // 2
    core = lax.axis_index("loop") % 2
    x = lax.axis_index("red") % RING
    place = jnp.stack([core, x]).astype(jnp.int32)
    swap = [(i, i ^ 1) for i in range(loops)]
    flip = [(i, (i + RING) % reds) for i in range(reds)]
    shift = [[(i, i - i % RING + (i + d) % RING) for i in range(reds)] for d in range(RING)]
    same_core = [[2 * i + c for i in range(chips)] for c in range(2)]

    def exchange(value):
        value = value.reshape(chips, -1, value.shape[-1])
        return lax.all_to_all(value, "loop", 0, 0, axis_index_groups=same_core)

    got = lax.ppermute(gradient, "loop", swap)
    sel = select(query_ids, out_basis, chips)
    sel_got = lax.ppermute(sel, "loop", swap)
    part = partial_rows(place, sel, sel_got, gradient, got)
    part = exchange(part)
    eigen_rows = jnp.take(jnp.take(out_eigen, layer_index, axis=0)[0], query_ids)
    eigen_rows = eigen_rows.reshape(chips, 2, CHUNKS, -1).transpose(2, 1, 0, 3).reshape(CHUNKS, chunk)
    eigen_cols = jnp.take(in_eigen, layer_index, axis=0)
    factors = [
        lax.dynamic_slice_in_dim(eigen_rows[n], x * piece, piece, 0)[:, None] for n in range(CHUNKS)
    ]
    rows_w, *factors = tie(add_up(part).astype(BF16), *factors)
    share = rows_w.shape[0] // CHUNKS

    def copied(rows):
        return jnp.broadcast_to(rows[None], (chips,) + rows.shape).reshape(chunk, half)

    def ring(parts):
        return [parts[0]] + [lax.ppermute(parts[d], "red", shift[d]) for d in range(1, RING)]

    def swapped(value):
        return lax.ppermute(value, "loop", swap)

    own_a = exchange(copied(rows_w[:share])).reshape(chunk, half)
    rows_b, own_a = tie(copied(rows_w[share:]), own_a)
    own_b = exchange(rows_b).reshape(chunk, half)
    rot_a = list(rotate(place, own_a, swapped(own_a), in_basis))
    own_b, rot_a[0] = tie(own_b, rot_a[0])
    ring_a = ring(rot_a)
    ring_b = ring(rotate(place, own_b, swapped(own_b), in_basis))
    total_a, rounded_a = ring_sum(ring_a)
    total_a, *ring_b = tie(total_a, *ring_b)
    far_a = lax.ppermute(rounded_a, "red", flip)
    total_b, rounded_b = ring_sum(ring_b)
    far_a, total_b = tie(far_a, total_b)
    scaled_a = scale(total_a, far_a, factors[0], eigen_cols)
    pieces_a = ring([scaled_a] * RING)
    far_b = lax.ppermute(rounded_b, "red", flip)
    scaled_b = scale(total_b, far_b, factors[1], eigen_cols)
    pieces_b = ring([scaled_b] * RING)
    send_a, keep_a = back(place, pieces_a, in_basis)
    pieces_b[0], send_a = tie(pieces_b[0], send_a)
    send_b, keep_b = back(place, pieces_b, in_basis)
    part = join([keep_a, swapped(send_a), keep_b, swapped(send_b)], chips)
    return add_up(exchange(part)).astype(BF16)


def solution(mesh):
    return jax.shard_map(
        per_device,
        mesh=mesh,
        in_specs=(
            P(),
            P(),
            P("loop", "red"),
            P("loop", None),
            P("red", "loop"),
            P(),
            P(None, "loop"),
        ),
        out_specs=P("loop", "red"),
        check_vma=False,
    )
```
